32 devices in a mesh: row: 4 (over z), col: 8 (over y, x, core).
Axes of the slice: x: 2, y: 2, z: 4, core: 2. Of those that a mesh axis runs over, the one named last changes fastest.
Arguments:
- inverse_top: bfloat16 [1024, 1024], P('col', 'row'), may hold values from -0.1875 to 0.1875
- inverse_one: bfloat16 [1536, 768], P('col', 'row'), may hold values from -0.21875 to 0.21875
- inverse_two: bfloat16 [2048, 512], P('col', 'row'), may hold values from -0.25 to 0.25
- inverse_leaf: bfloat16 [2048, 256], P('col', 'row'), may hold values from -0.375 to 0.375
- coupling_one: bfloat16 [768, 1536], P('row', 'col'), may hold values from -0.21875 to 0.21875
- coupling_two: bfloat16 [512, 2048], P('row', 'col'), may hold values from -0.25 to 0.25
- coupling_leaf: bfloat16 [256, 2048], P('row', 'col'), may hold values from -0.375 to 0.375
- rhs_top: bfloat16 [1024, 256], P('row', 'col'), may hold values from -6 to 6
- rhs_one: bfloat16 [768, 512], P('row', 'col'), may hold values from -6 to 6
- rhs_two: bfloat16 [512, 1024], P('row', 'col'), may hold values from -6 to 6
- rhs_leaf: bfloat16 [256, 2048], P('row', 'col'), may hold values from -6 to 6
- parent_map_one: int32 [2, 768], replicated, may hold values from 0 to 1023, as said below
- parent_map_two: int32 [4, 512], replicated, may hold values from 0 to 1535, as said below
- parent_map_leaf: int32 [8, 256], replicated, may hold values from 0 to 1023, as said below
Outputs:
- solution_top: bfloat16 [1024, 256], P('row', 'col')
- solution_one: bfloat16 [768, 512], P('row', 'col')
- solution_two: bfloat16 [512, 1024], P('row', 'col')
- solution_leaf: bfloat16 [256, 2048], P('row', 'col')
The draws below stay inside these ranges and needn't reach their ends.
Inputs may be any that keep to these rules, and one draw needn't show every extreme that they name: `parent_map_one`: row k lists distinct rows of the top front, one for each of the 768 update rows of front k. Cut the update rows and the top separator each into 4 equal blocks: at most 96 rows of one block land in one block of the top front, a number that is reached in every row, and every block of the top front receives exactly 192 rows from each child. `parent_map_two`: row k lists distinct rows of the front k // 2 of the second level (its 768 separator rows first, then its 768 update rows), one for each of the 512 update rows of front k. Cut the update rows into 4 equal blocks, and the parent's separator rows and its update rows each into 4 equal blocks, block j of the parent being the j-th separator block with the j-th update block: at most 64 rows of one block land in one parent block, reached in every row, and every parent block receives exactly 128 rows from each child. `parent_map_leaf`: as for parent_map_two, one level lower: 256 update rows of front k into front k // 2 of the third level, at most 32 rows of one block into one parent block, reached in every row, and exactly 64 rows from each child into every parent block.
All inputs are finite; a program needn't handle non-finite values.
Results may differ from the reference program's by a relative error of at most 0.03.
Values may be sent and summed in bfloat16 or wider, within the bound.
A program may use at most 64 MiB of HBM per device.

```python
import jax
import jax.numpy as jnp
from jax import lax

COLUMNS = 256
STRIPS = 4
SEP_TOP = 1024
SEP_ONE = 768
SEP_TWO = 512
SEP_LEAF = 256


def level_map(key, fronts, upd_order, sep_parent, upd_parent):
    strips = STRIPS
    block_rows = upd_order // strips
    mean_load = upd_order // (strips * strips)
    block_len = (sep_parent + upd_parent) // strips
    sep_rows = sep_parent // strips
    upd_rows = max(upd_parent // strips, 1)

    def one_child(child_key):
        subkeys = jax.random.split(child_key, 4)
        pairing = jax.random.permutation(subkeys[0], strips)
        swings = jax.random.randint(subkeys[1], (strips // 2,), 0, mean_load + 1).astype(jnp.int32)
        swings = swings.at[0].set(mean_load)
        shifts = jnp.zeros((strips,), jnp.int32).at[pairing[0::2]].set(swings).at[pairing[1::2]].set(-swings)
        source = jnp.arange(strips, dtype=jnp.int32)[:, None]
        target = jnp.arange(strips, dtype=jnp.int32)[None, :]
        load_table = mean_load + shifts[(target - source) % strips]
        load_ends = jnp.cumsum(load_table, axis=1)
        local_at = jnp.arange(block_rows, dtype=jnp.int32)
        target_of = jnp.sum((load_ends[:, None, :] <= local_at[None, :, None]).astype(jnp.int32), axis=2)
        starts = load_ends - load_table
        slot_of = local_at[None, :] - jnp.take_along_axis(starts, target_of, axis=1)
        before = jnp.cumsum(load_table, axis=0) - load_table
        rank_of = jnp.take_along_axis(before, target_of, axis=1) + slot_of
        orders = jax.vmap(lambda subkey: jax.random.permutation(subkey, block_len))(jax.random.split(subkeys[2], strips))
        placed = orders[target_of, rank_of]
        values = jnp.where(placed < sep_rows, target_of * sep_rows + placed, sep_parent + target_of * upd_rows + placed - sep_rows)
        shuffles = jax.vmap(lambda subkey: jax.random.permutation(subkey, block_rows))(jax.random.split(subkeys[3], strips))
        result = jnp.zeros((strips, block_rows), jnp.int32).at[jnp.arange(strips)[:, None], shuffles].set(values.astype(jnp.int32))
        return result.reshape(upd_order).astype(jnp.int32)
    return jax.vmap(one_child)(jax.random.split(key, fronts))


def draw_parent_map_one(key, part):
    return level_map(jax.random.fold_in(key, 11), 2, SEP_ONE, SEP_TOP, 0)


def draw_parent_map_two(key, part):
    return level_map(jax.random.fold_in(key, 12), 4, SEP_TWO, SEP_ONE, SEP_ONE)


def draw_parent_map_leaf(key, part):
    return level_map(jax.random.fold_in(key, 13), 8, SEP_LEAF, SEP_TWO, SEP_TWO)


def block_scale(key, extent, cuts, low, largest):
    loudness, own = 1.0, jax.random.fold_in(key, 6)
    for position, parts in cuts:
        draws = jnp.exp(jax.random.uniform(jax.random.fold_in(own, position), (parts,), jnp.float32, low / len(cuts), largest / len(cuts)))
        loudness = loudness * jnp.repeat(draws, extent[position] // parts).reshape([-1 if axis == position else 1 for axis in range(len(extent))])
    return loudness


def gaussian(key, shape, scale, reach, cuts=(), kind=jnp.bfloat16):
    gain = block_scale(key, shape, cuts, -0.22, 0.18) if cuts else 1.0
    array = jax.random.normal(key, shape, jnp.float32) * scale * gain
    return jnp.minimum(jnp.maximum(array, -reach), reach).astype(kind)


def setup_inputs(seed: int = 0) -> dict:
    keys = jax.random.split(jax.random.key(seed), 15)
    return {
        "inverse_top": gaussian(keys[0], (SEP_TOP, SEP_TOP), SEP_TOP ** -0.5, 0.1875, ((0, 8), (1, 4))),
        "inverse_one": gaussian(keys[1], (2 * SEP_ONE, SEP_ONE), SEP_ONE ** -0.5, 0.21875, ((0, 8), (1, 4))),
        "inverse_two": gaussian(keys[2], (4 * SEP_TWO, SEP_TWO), SEP_TWO ** -0.5, 0.25, ((0, 8), (1, 4))),
        "inverse_leaf": gaussian(keys[3], (8 * SEP_LEAF, SEP_LEAF), SEP_LEAF ** -0.5, 0.375, ((0, 8), (1, 4))),
        "coupling_one": gaussian(keys[4], (SEP_ONE, 2 * SEP_ONE), SEP_ONE ** -0.5, 0.21875, ((0, 4), (1, 8))),
        "coupling_two": gaussian(keys[5], (SEP_TWO, 4 * SEP_TWO), SEP_TWO ** -0.5, 0.25, ((0, 4), (1, 8))),
        "coupling_leaf": gaussian(keys[6], (SEP_LEAF, 8 * SEP_LEAF), SEP_LEAF ** -0.5, 0.375, ((0, 4), (1, 8))),
        "rhs_top": gaussian(keys[7], (SEP_TOP, COLUMNS), 1.0, 6.0, ((0, 4), (1, 8))),
        "rhs_one": gaussian(keys[8], (SEP_ONE, 2 * COLUMNS), 1.0, 6.0, ((0, 4), (1, 8))),
        "rhs_two": gaussian(keys[9], (SEP_TWO, 4 * COLUMNS), 1.0, 6.0, ((0, 4), (1, 8))),
        "rhs_leaf": gaussian(keys[10], (SEP_LEAF, 8 * COLUMNS), 1.0, 6.0, ((0, 4), (1, 8))),
        "parent_map_one": draw_parent_map_one(jax.random.fold_in(keys[14], 71), 0),
        "parent_map_two": draw_parent_map_two(jax.random.fold_in(keys[14], 71), 0),
        "parent_map_leaf": draw_parent_map_leaf(jax.random.fold_in(keys[14], 71), 0),
    }


def pivot_product(inverse, vector):
    strip_width = inverse.shape[1] // STRIPS
    summed = jnp.zeros((inverse.shape[0], vector.shape[1]), jnp.float32)
    for strip_at in range(STRIPS):
        low_edge = strip_at * strip_width
        partial_value = jnp.dot(inverse[:, low_edge:low_edge + strip_width], vector[low_edge:low_edge + strip_width], preferred_element_type=jnp.float32)
        summed = summed + lax.optimization_barrier(partial_value.astype(jnp.bfloat16)).astype(jnp.float32)
    return summed


def coupling_back(coupling, gathered):
    strip_width = coupling.shape[0] // STRIPS
    summed = jnp.zeros((coupling.shape[1], gathered.shape[1]), jnp.float32)
    for strip_at in range(STRIPS):
        low_edge = strip_at * strip_width
        partial_value = jnp.dot(coupling[low_edge:low_edge + strip_width].T, gathered[low_edge:low_edge + strip_width], preferred_element_type=jnp.float32)
        summed = summed + lax.optimization_barrier(partial_value.astype(jnp.bfloat16)).astype(jnp.float32)
    return summed


def reference(inverse_top, inverse_one, inverse_two, inverse_leaf, coupling_one, coupling_two, coupling_leaf, rhs_top, rhs_one, rhs_two, rhs_leaf, parent_map_one, parent_map_two, parent_map_leaf):
    inverses = [inverse_top, inverse_one, inverse_two, inverse_leaf]
    couplings = [None, coupling_one, coupling_two, coupling_leaf]
    right_sides = [rhs_top, rhs_one, rhs_two, rhs_leaf]
    parent_maps = [None, parent_map_one, parent_map_two, parent_map_leaf]
    orders = [SEP_TOP, SEP_ONE, SEP_TWO, SEP_LEAF]
    pivots = [[None] * (2 ** tree_level) for tree_level in range(4)]
    updates = [[None] * (2 ** tree_level) for tree_level in range(4)]
    for tree_level in (3, 2, 1, 0):
        sep_order = orders[tree_level]
        for front_at in range(2 ** tree_level):
            right_side = right_sides[tree_level][:, front_at * COLUMNS:(front_at + 1) * COLUMNS]
            if tree_level == 3:
                separator = right_side
                update = jnp.zeros((sep_order, COLUMNS), jnp.bfloat16)
            else:
                length = sep_order + (sep_order if tree_level > 0 else 0)
                extended = jnp.zeros((length, COLUMNS), jnp.float32)
                for child_at in (2 * front_at, 2 * front_at + 1):
                    extended = extended.at[parent_maps[tree_level + 1][child_at]].add(updates[tree_level + 1][child_at].astype(jnp.float32))
                separator = (right_side.astype(jnp.float32) + extended[:sep_order]).astype(jnp.bfloat16)
                update = lax.optimization_barrier(extended[sep_order:].astype(jnp.bfloat16))
            inverse = inverses[tree_level][front_at * sep_order:(front_at + 1) * sep_order]
            pivot_out = pivot_product(inverse, separator).astype(jnp.bfloat16)
            pivots[tree_level][front_at] = pivot_out
            if tree_level > 0:
                coupling = couplings[tree_level][:, front_at * sep_order:(front_at + 1) * sep_order]
                coupled = jnp.dot(coupling, pivot_out, preferred_element_type=jnp.float32)
                updates[tree_level][front_at] = (update.astype(jnp.float32) - coupled).astype(jnp.bfloat16)
    solutions = [[None] * (2 ** tree_level) for tree_level in range(4)]
    gathered_rows = [[None] * (2 ** tree_level) for tree_level in range(4)]
    for tree_level in range(4):
        sep_order = orders[tree_level]
        for front_at in range(2 ** tree_level):
            pivot_out = pivots[tree_level][front_at]
            if tree_level == 0:
                residual = pivot_out
            else:
                parent_at = front_at // 2
                pieces = [solutions[tree_level - 1][parent_at]]
                if tree_level > 1:
                    pieces.append(gathered_rows[tree_level - 1][parent_at])
                parent_rows = jnp.concatenate(pieces, axis=0)
                gathered = parent_rows[parent_maps[tree_level][front_at]]
                gathered_rows[tree_level][front_at] = gathered
                coupling = couplings[tree_level][:, front_at * sep_order:(front_at + 1) * sep_order]
                residual = (pivot_out.astype(jnp.float32) - coupling_back(coupling, gathered)).astype(jnp.bfloat16)
            inverse = inverses[tree_level][front_at * sep_order:(front_at + 1) * sep_order]
            solutions[tree_level][front_at] = jnp.dot(inverse.T, residual, preferred_element_type=jnp.float32).astype(jnp.bfloat16)
    outputs = [jnp.concatenate(solutions[tree_level], axis=1) for tree_level in range(4)]
    return (outputs[0], outputs[1], outputs[2], outputs[3])
```

```python
import jax
import jax.numpy as jnp
from jax import lax
from jax.experimental import pallas as pl
from jax.experimental.pallas import tpu as pltpu
from jax.sharding import PartitionSpec as P


def swapped(value, axis, stride):
    mask = 2**stride
    pairs = [(source, source ^ mask) for source in range(lax.axis_size(axis))]
    return lax.ppermute(value, axis, pairs)


def route_tables(mapping, child_index, parent_sep, parent_upd, strips, row_index):
    positions = lax.dynamic_index_in_dim(mapping, child_index, 0, keepdims=False)
    sep_rows = parent_sep // strips
    in_separator = positions < parent_sep
    if parent_upd > 0:
        upd_rows = parent_upd // strips
        target = jnp.where(
            in_separator, positions // sep_rows, (positions - parent_sep) // upd_rows
        )
        offset = jnp.where(
            in_separator, positions % sep_rows, sep_rows + (positions - parent_sep) % upd_rows
        )
    else:
        target = positions // sep_rows
        offset = positions % sep_rows
    block_rows = positions.shape[0] // strips
    blocks = target.reshape(strips, block_rows)
    matches = (blocks[:, :, None] == jnp.arange(strips, dtype=jnp.int32)[None, None, :]).astype(
        jnp.int32
    )
    slot_of = jnp.sum((jnp.cumsum(matches, axis=1) - 1) * matches, axis=2).reshape(-1)
    block_len = sep_rows + parent_upd // strips
    capacity = 2 * positions.shape[0] // (strips * strips)
    source = jnp.arange(positions.shape[0], dtype=jnp.int32) // block_rows
    mine_here = target == row_index
    column_at = jnp.where(mine_here, slot_of, capacity)
    lookup = jnp.full((strips, capacity + 1), block_len, jnp.int32)
    lookup = lookup.at[source, column_at].set(jnp.where(mine_here, offset, block_len))[:, :capacity]
    local_target = lax.dynamic_slice_in_dim(target, row_index * block_rows, block_rows)
    local_slots = lax.dynamic_slice_in_dim(slot_of, row_index * block_rows, block_rows)
    return (local_target, local_slots, lookup, capacity, block_len)


def pack_rows(values, local_target, local_slots, strips, capacity):
    buffer = jnp.zeros((strips, capacity, values.shape[1]), values.dtype)
    return buffer.at[local_target, local_slots].set(values)


def unpack_rows(received, lookup, block_len):
    summed = jnp.zeros((block_len + 1, received.shape[2]), jnp.float32)
    return summed.at[lookup].add(received.astype(jnp.float32))[:block_len]


def spread(portion, depth_bits, pass_on, column):
    for bit_index in range(depth_bits):
        partner = pass_on(portion, bit_index)
        is_upper = column >> bit_index & 1 == 1
        portion = jnp.where(
            is_upper,
            jnp.concatenate([partner, portion], axis=-1),
            jnp.concatenate([portion, partner], axis=-1),
        )
    return portion


def shrink(entire, depth_bits, pass_on, column):
    for bit_index in reversed(range(depth_bits)):
        half_width = entire.shape[-1] // 2
        low_part = entire[..., :half_width]
        high_part = entire[..., half_width:]
        is_upper = column >> bit_index & 1 == 1
        kept_part = jnp.where(is_upper, high_part, low_part)
        sent_part = jnp.where(is_upper, low_part, high_part)
        entire = kept_part + pass_on(sent_part, bit_index)
    return entire


def per_device(
    inverse_top,
    inverse_one,
    inverse_two,
    inverse_leaf,
    coupling_one,
    coupling_two,
    coupling_leaf,
    rhs_top,
    rhs_one,
    rhs_two,
    rhs_leaf,
    parent_map_one,
    parent_map_two,
    parent_map_leaf,
):
    strips = lax.axis_size("row")
    col_count = lax.axis_size("col")
    row_here = lax.axis_index("row")
    column = lax.axis_index("col")
    inverses = [inverse_top, inverse_one, inverse_two, inverse_leaf]
    couplings = [None, coupling_one, coupling_two, coupling_leaf]
    right_sides = [rhs_top, rhs_one, rhs_two, rhs_leaf]
    parent_maps = [None, parent_map_one, parent_map_two, parent_map_leaf]
    orders = [inverse.shape[1] * strips for inverse in inverses]
    groups = [col_count >> tree_level for tree_level in range(4)]
    group_bits = [group_size.bit_length() - 1 for group_size in groups]
    pass_rhs = lambda values, bit_index: swapped(values, "col", bit_index)
    pass_update_sum = lambda values, bit_index: swapped(
        values.astype(jnp.bfloat16), "col", bit_index
    ).astype(values.dtype)
    pass_update_spread = lambda values, bit_index: swapped(values, "col", bit_index)
    pass_solution_sum = lambda values, bit_index: swapped(
        values.astype(jnp.bfloat16), "col", bit_index
    ).astype(values.dtype)
    pass_solution_spread = lambda values, bit_index: swapped(values, "col", bit_index)
    full_rhs = [
        spread(right_sides[tree_level], group_bits[tree_level], pass_rhs, column)
        for tree_level in range(4)
    ]
    own_routes = [None]
    for tree_level in range(1, 4):
        parent_order = orders[tree_level - 1]
        parent_update = parent_order if tree_level > 1 else 0
        front_here = column // groups[tree_level]
        own_routes.append(
            route_tables(
                parent_maps[tree_level], front_here, parent_order, parent_update, strips, row_here
            )
        )
    pivots = [None] * 4
    incoming = None
    for tree_level in (3, 2, 1, 0):
        sep_rows = inverses[tree_level].shape[1]
        if incoming is None:
            separator = full_rhs[tree_level]
            own_update = None
        else:
            separator = (full_rhs[tree_level].astype(jnp.float32) + incoming[:sep_rows]).astype(
                jnp.bfloat16
            )
            own_update = lax.optimization_barrier(incoming[sep_rows:].astype(jnp.bfloat16))
        partial_value = jnp.dot(inverses[tree_level], separator, preferred_element_type=jnp.float32)
        solved = lax.psum(partial_value.astype(jnp.bfloat16), "row")
        pivots[tree_level] = solved
        if tree_level > 0:
            coupled = jnp.dot(couplings[tree_level], solved, preferred_element_type=jnp.float32)
            reduced = shrink(coupled, group_bits[tree_level], pass_update_sum, column)
            if own_update is None:
                portion = (-reduced).astype(jnp.bfloat16)
            else:
                start_at = column % groups[tree_level] * reduced.shape[1]
                kept_rows = lax.dynamic_slice_in_dim(own_update, start_at, reduced.shape[1], 1)
                portion = (kept_rows.astype(jnp.float32) - reduced).astype(jnp.bfloat16)
            updated = spread(portion, group_bits[tree_level], pass_update_spread, column)
            own_target, own_slots, own_lookup, capacity, block_len = own_routes[tree_level]
            got_own = lax.all_to_all(
                pack_rows(updated, own_target, own_slots, strips, capacity),
                "row",
                split_axis=0,
                concat_axis=0,
                tiled=True,
            )
            own_part = unpack_rows(got_own, own_lookup, block_len)
            partner = swapped(own_part.astype(jnp.bfloat16), "col", group_bits[tree_level])
            incoming = own_part + partner.astype(jnp.float32)
    solutions = [None] * 4
    parent_solution = None
    parent_gathered = None
    for tree_level in range(4):
        solved = pivots[tree_level]
        gathered = None
        if tree_level == 0:
            residual = solved
        else:
            own_target, own_slots, own_lookup, capacity, block_len = own_routes[tree_level]
            pieces = [parent_solution]
            if parent_gathered is not None:
                pieces.append(parent_gathered)
            pieces.append(jnp.zeros((1, parent_solution.shape[1]), jnp.bfloat16))
            parent_rows = jnp.concatenate(pieces, axis=0)
            returned = lax.all_to_all(
                parent_rows[own_lookup], "row", split_axis=0, concat_axis=0, tiled=True
            )
            gathered = returned[own_target, own_slots]
            coupling_term = jnp.dot(
                couplings[tree_level].T, gathered, preferred_element_type=jnp.float32
            )
            residual = (
                solved.astype(jnp.float32)
                - lax.psum(coupling_term.astype(jnp.bfloat16), "row").astype(jnp.float32)
            ).astype(jnp.bfloat16)
        contribution = jnp.dot(inverses[tree_level].T, residual, preferred_element_type=jnp.float32)
        if tree_level == 0:
            summed = lax.psum(contribution.astype(jnp.bfloat16), "col")
            solution = summed
            rhs_width = solution.shape[1] // groups[0]
            solutions[0] = lax.dynamic_slice_in_dim(
                solution, column % groups[0] * rhs_width, rhs_width, 1
            )
        else:
            portion = shrink(
                contribution, group_bits[tree_level], pass_solution_sum, column
            ).astype(jnp.bfloat16)
            solutions[tree_level] = portion
            if tree_level < 3:
                solution = spread(portion, group_bits[tree_level], pass_solution_spread, column)
        parent_solution = solution
        parent_gathered = gathered
    return (solutions[0], solutions[1], solutions[2], solutions[3])


MESH = pl.DeviceIdType.MESH


def dot_nn(left, right):
    return lax.dot_general(left, right, (((1,), (0,)), ((), ())), preferred_element_type=jnp.float32)


def dot_nt(left, right):
    return lax.dot_general(left, right, (((1,), (1,)), ((), ())), preferred_element_type=jnp.float32)


def eye(size):
    rows = lax.broadcasted_iota(jnp.int32, (size, size), 0)
    columns = lax.broadcasted_iota(jnp.int32, (size, size), 1)
    return jnp.where(rows == columns, 1.0, 0.0).astype(jnp.bfloat16)


def flipped(value, mask):
    result = value
    bit = 1
    while bit <= mask:
        if mask & bit:
            result = result + bit * (1 - 2 * ((value // bit) % 2))
        bit *= 2
    return result


class Plan:
    def __init__(self, rows, cols, inverse_shapes, rhs_top_shape):
        self.rows, self.cols = rows, cols
        self.strip = [shape[1] for shape in inverse_shapes]
        self.order = [shape[1] * rows for shape in inverse_shapes]
        self.local = [shape[0] for shape in inverse_shapes]
        self.group = [cols >> level for level in range(4)]
        self.columns = rhs_top_shape[1] * cols
        self.width = [self.columns // group if group else 0 for group in self.group]
        self.mine = self.columns // rows

    def total(self, level):
        return self.order[level] * (2 if level else 1)

    def fits(self):
        table = sum(
            2 * self.total(level) * self.order[level + 1] * 2 for level in range(3)
        )
        if self.group[3] != 1 or self.mine * self.rows != self.columns or table > 24 * 2**20:
            return False
        for level in range(4):
            if self.strip[level] % 16 or self.order[level] % 128 or self.width[level] % 16:
                return False
            if max(self.width[level], self.mine) % min(self.width[level], self.mine):
                return False
        for level in (1, 2):
            if self.mine % (16 * self.group[level]):
                return False
        return self.order[0] % (128 * self.group[0]) == 0 and self.group[0] % self.rows == 0


def build_kernel(plan):
    R, CC, N = plan.rows, plan.cols, plan.mine
    S, K, L, G, W = plan.order, plan.strip, plan.local, plan.group, plan.width
    bf = jnp.bfloat16
    scratch, names = [], {}

    def ref(name, shape, dtype=bf):
        names[name] = len(scratch)
        scratch.append(pltpu.VMEM(shape, dtype))

    def sems(name, shape):
        names[name] = len(scratch)
        scratch.append(pltpu.SemaphoreType.DMA(shape))

    for l in range(4):
        n_dest = max(1, W[l] // N)
        n_part = max(1, N // W[l])
        ref(f"Z{l}", (R, L[l], K[l]))
        sems(f"Zs{l}", (R,))
        sems(f"Zr{l}", (R,))
        if l:
            ref(f"C{l}", (S[l], L[l]))
            sems(f"Cs{l}", (R,))
            sems(f"Cr{l}", (R,))
        ref(f"bT{l}", (W[l], K[l]))
        ref(f"B{l}", (R, N, K[l]))
        sems(f"Bs{l}", (n_dest, G[l]))
        sems(f"Br{l}", (R, n_part))
        ref(f"y{l}", (N, L[l]))
        ref(f"fx{l}", (R, N, K[l]))
        ref(f"oT{l}", (W[l], K[l]))
        sems(f"Os{l}", (R,))
        sems(f"Or{l}", (n_dest,))
        if l < 3:
            ref(f"hot{l}", (2, plan.total(l), S[l + 1]))
            if l:
                shape = (G[l], R, N // G[l], K[l])
                ref(f"xp{l}", shape)
                ref(f"xr{l}", shape)
                ref(f"xs{l}", shape)
            else:
                shape = (G[0], N, S[0] // G[0])
                ref("xp0", shape)
                ref("xr0", shape)
                ref("xs0", shape)
            for tag in ("xps", "xpr", "xss", "xsr"):
                sems(f"{tag}{l}", (G[l],))
        if l:
            shape = (G[l], N // G[l], S[l])
            ref(f"u{l}", (2,) + shape)
            sems(f"us{l}", (2 * G[l],))
            sems(f"ur{l}", (2 * G[l],))
            ref(f"v{l}", (N, S[l]))
            if G[l] > 1:
                ref(f"H{l}", shape)
                ref(f"up{l}", shape)
                ref(f"ut{l}", shape)
                sems(f"ups{l}", (G[l],))
                sems(f"upr{l}", (G[l],))

    def kernel(*refs):
        inverse = refs[0:4]
        coupling = (None,) + tuple(refs[4:7])
        rhs = refs[7:11]
        maps = (None,) + tuple(refs[11:14])
        outs = refs[14:18]
        held = refs[18:]
        at = lambda name: held[names[name]]
        z = lax.axis_index("row")
        c = lax.axis_index("col")
        sent = []

        def remote(src, dst, ssem, rsem, z_to, c_to):
            return pltpu.make_async_remote_copy(
                src_ref=src, dst_ref=dst, send_sem=ssem, recv_sem=rsem,
                device_id=(z_to, c_to), device_id_type=MESH,
            )

        def send(src, dst, ssem, rsem, z_to, c_to):
            copy = remote(src, dst, ssem, rsem, z_to, c_to)
            copy.start()
            sent.append(copy.wait_send)

        def send_or_copy(src, dst, ssem, rsem, z_to, c_to, here):
            @pl.when(here)
            def _():
                pltpu.make_async_copy(src, dst, rsem).start()

            @pl.when(jnp.logical_not(here))
            def _():
                remote(src, dst, ssem, rsem, z_to, c_to).start()

            def finish():
                @pl.when(jnp.logical_not(here))
                def _():
                    remote(src, dst, ssem, rsem, z_to, c_to).wait_send()

            sent.append(finish)

        def arrived(dst, rsem):
            pltpu.make_async_copy(dst, dst, rsem).wait()

        barrier = pltpu.get_barrier_semaphore()
        for dz in range(R):
            for m in range(CC):
                if dz or m:
                    pl.semaphore_signal(
                        barrier, inc=1, device_id=((z + dz) % R, flipped(c, m)),
                        device_id_type=MESH,
                    )
        for l in range(4):
            at(f"bT{l}")[...] = dot_nt(eye(W[l]), rhs[l][...]).astype(bf)
        pl.semaphore_wait(barrier, R * CC - 1)

        def start_rhs(l):
            q = c % G[l]
            n_dest, n_part = max(1, W[l] // N), max(1, N // W[l])
            for i in range(n_dest):
                if W[l] >= N:
                    z_to = q * n_dest + i
                    src = at(f"bT{l}").at[pl.ds(i * N, N)]
                    dst = at(f"B{l}").at[z]
                    part = 0
                else:
                    z_to = q // n_part
                    part = q % n_part
                    src = at(f"bT{l}")
                    dst = at(f"B{l}").at[z, pl.ds(pl.multiple_of(part * W[l], W[l]), W[l])]
                for m in range(G[l]):
                    ssem, rsem = at(f"Bs{l}").at[i, m], at(f"Br{l}").at[z, part]
                    if m:
                        send(src, dst, ssem, rsem, z_to, flipped(c, m))
                    else:
                        send_or_copy(src, dst, ssem, rsem, z_to, c, z_to == z)

        def wait_rhs(l):
            n_part = max(1, N // W[l])
            for s in range(R):
                for part in range(n_part):
                    if n_part > 1:
                        dst = at(f"B{l}").at[s, pl.ds(part * W[l], W[l])]
                    else:
                        dst = at(f"B{l}").at[s]
                    arrived(dst, at(f"Br{l}").at[s, part])

        def c_rows(l, index):
            return at(f"C{l}").at[pl.ds(pl.multiple_of(index * K[l], 16), K[l])]

        def start_weights(l):
            pltpu.make_async_copy(inverse[l], at(f"Z{l}").at[z], at(f"Zr{l}").at[0]).start()
            if l:
                pltpu.make_async_copy(coupling[l], c_rows(l, z), at(f"Cr{l}").at[0]).start()
            for d in range(1, R):
                z_to = (z + d) % R
                send(inverse[l], at(f"Z{l}").at[z], at(f"Zs{l}").at[d], at(f"Zr{l}").at[d], z_to, c)
                if l:
                    send(coupling[l], c_rows(l, z), at(f"Cs{l}").at[d], at(f"Cr{l}").at[d], z_to, c)

        def wait_inverse(l):
            for d in range(R):
                arrived(at(f"Z{l}").at[(z + R - d) % R], at(f"Zr{l}").at[d])

        def wait_coupling(l):
            for d in range(R):
                arrived(c_rows(l, (z + R - d) % R), at(f"Cr{l}").at[d])

        def scatter(name, l, landed, ssem, rsem):
            q = c % G[l]
            for m in range(1, G[l]):
                send(
                    at(name).at[flipped(q, m)], at(landed).at[m],
                    at(ssem).at[m], at(rsem).at[m], z, flipped(c, m),
                )

        def total(name, l, landed, rsem):
            value = at(name)[c % G[l]].astype(jnp.float32)
            for m in range(1, G[l]):
                arrived(at(landed).at[m], at(rsem).at[m])
                value = value + at(landed)[m].astype(jnp.float32)
            return value

        def share_solution(l):
            q = c % G[l]
            here = at(f"xs{l}").at[q]
            for m in range(1, G[l]):
                send(here, here, at(f"xss{l}").at[m], at(f"xsr{l}").at[m], z, flipped(c, m))

        def wait_solution(l):
            q = c % G[l]
            for m in range(1, G[l]):
                arrived(at(f"xs{l}").at[flipped(q, m)], at(f"xsr{l}").at[m])

        def share_update(l):
            child, q = (c // G[l]) % 2, c % G[l]
            here = at(f"u{l}").at[child, q]
            for m in range(1, 2 * G[l]):
                send(here, here, at(f"us{l}").at[m], at(f"ur{l}").at[m], z, flipped(c, m))

        def wait_update(l):
            for m in range(1, 2 * G[l]):
                other = flipped(c, m)
                arrived(
                    at(f"u{l}").at[(other // G[l]) % 2, other % G[l]], at(f"ur{l}").at[m]
                )

        def make_table(l):
            front = c // G[l]
            step = K[l]
            for child in range(2):
                row = maps[l + 1][pl.ds(2 * front + child, 1), :]

                def body(i, carry):
                    start = pl.multiple_of(i * step, 16)
                    at_row = lax.broadcasted_iota(jnp.int32, (step, S[l + 1]), 0) + start
                    at(f"hot{l}")[child, pl.ds(start, step), :] = jnp.where(
                        at_row == row, 1.0, 0.0
                    ).astype(bf)
                    return carry

                lax.fori_loop(0, plan.total(l) // step, body, 0)

        def start_out(l):
            q = c % G[l]
            n_dest, n_part = max(1, W[l] // N), max(1, N // W[l])
            if W[l] >= N:
                holds = z // n_dest == q
                index = z % n_dest
                dst = at(f"oT{l}").at[pl.ds(pl.multiple_of(index * N, N), N)]
            else:
                holds = q // n_part == z
                index = 0
                dst = at(f"oT{l}")

            def piece(r):
                if W[l] >= N:
                    return at(f"fx{l}").at[r]
                low = pl.multiple_of((q % n_part) * W[l], W[l])
                return at(f"fx{l}").at[r, pl.ds(low, W[l])]

            def copy_to(d):
                r = (z + d) % R
                return remote(
                    piece(r), dst, at(f"Os{l}").at[d], at(f"Or{l}").at[index], r, c
                )

            @pl.when(holds)
            def _():
                pltpu.make_async_copy(piece(z), dst, at(f"Or{l}").at[index]).start()
                for d in range(1, R):
                    copy_to(d).start()

            def finish():
                @pl.when(holds)
                def _():
                    for d in range(1, R):
                        copy_to(d).wait_send()

            sent.append(finish)

        def finish_out(l):
            if W[l] >= N:
                for i in range(W[l] // N):
                    arrived(at(f"oT{l}").at[pl.ds(i * N, N)], at(f"Or{l}").at[i])
            else:
                arrived(at(f"oT{l}"), at(f"Or{l}").at[0])
            outs[l][...] = dot_nt(eye(K[l]), at(f"oT{l}")[...]).astype(bf)

        def pivot(l, blocks):
            value = dot_nt(blocks[0], at(f"Z{l}")[0])
            for r in range(1, R):
                value = value + dot_nt(blocks[r], at(f"Z{l}")[r])
            at(f"y{l}")[...] = value.astype(bf)

        start_rhs(3)
        start_weights(3)
        start_weights(2)
        start_rhs(2)
        make_table(2)
        wait_rhs(3)
        wait_inverse(3)
        pivot(3, [at("B3")[r] for r in range(R)])
        wait_coupling(3)
        at("u3")[(c // G[3]) % 2, 0] = (-dot_nt(at("y3")[...], at("C3")[...])).astype(bf)
        share_update(3)
        start_weights(1)
        start_rhs(1)
        make_table(1)

        for l in (2, 1, 0):
            wait_update(l + 1)
            pair = [at(f"u{l + 1}")[child].reshape(N, S[l + 1]) for child in range(2)]

            def assembled(low, size):
                value = dot_nt(pair[0], at(f"hot{l}")[0, low:low + size, :])
                return value + dot_nt(pair[1], at(f"hot{l}")[1, low:low + size, :])

            wait_rhs(l)
            blocks = [
                (at(f"B{l}")[r].astype(jnp.float32) + assembled(r * K[l], K[l])).astype(bf)
                for r in range(R)
            ]
            wait_inverse(l)
            pivot(l, blocks)
            if l:
                wait_coupling(l)
                share = (G[l], N // G[l], S[l])
                at(f"up{l}")[...] = (
                    dot_nt(at(f"y{l}")[...], at(f"C{l}")[...]).astype(bf).reshape(share)
                )
                scatter(f"up{l}", l, f"ut{l}", f"ups{l}", f"upr{l}")
                if l == 2:
                    start_weights(0)
                    start_rhs(0)
                    make_table(0)
                at(f"H{l}")[...] = assembled(S[l], S[l]).astype(bf).reshape(share)
                reduced = total(f"up{l}", l, f"ut{l}", f"upr{l}")
                q = c % G[l]
                at(f"u{l}")[(c // G[l]) % 2, q] = (
                    at(f"H{l}")[q].astype(jnp.float32) - reduced
                ).astype(bf)
                share_update(l)

        per = G[0] // R
        lanes = S[0] // G[0]
        for r in range(R):
            value = dot_nn(at("y0")[...], at("Z0")[r]).astype(bf)
            for i in range(per):
                at("xp0")[r * per + i] = value[:, i * lanes:(i + 1) * lanes]
        scatter("xp0", 0, "xr0", "xps0", "xpr0")
        at("xs0")[c % G[0]] = total("xp0", 0, "xr0", "xpr0").astype(bf)
        share_solution(0)
        wait_solution(0)
        for r in range(R):
            for i in range(per):
                at("fx0")[r, :, i * lanes:(i + 1) * lanes] = at("xs0")[r * per + i]
        start_out(0)

        for l in (1, 2, 3):
            child = (c // G[l]) % 2
            gathered = dot_nn(at(f"fx{l - 1}")[0], at(f"hot{l - 1}")[child, 0:K[l - 1], :])
            for r in range(1, R):
                gathered = gathered + dot_nn(
                    at(f"fx{l - 1}")[r],
                    at(f"hot{l - 1}")[child, r * K[l - 1]:(r + 1) * K[l - 1], :],
                )
            if l > 1:
                gathered = gathered + dot_nn(
                    at(f"v{l - 1}")[...], at(f"hot{l - 1}")[child, S[l - 1]:, :]
                )
            at(f"v{l}")[...] = gathered.astype(bf)
            residual = (
                at(f"y{l}")[...].astype(jnp.float32)
                - dot_nn(at(f"v{l}")[...], at(f"C{l}")[...])
            ).astype(bf)
            for r in range(R):
                value = dot_nn(residual, at(f"Z{l}")[r]).astype(bf)
                if G[l] > 1:
                    at(f"xp{l}")[:, r] = value.reshape(G[l], N // G[l], K[l])
                else:
                    at(f"fx{l}")[r] = value
            if G[l] > 1:
                scatter(f"xp{l}", l, f"xr{l}", f"xps{l}", f"xpr{l}")
                if l == 1:
                    finish_out(0)
                at(f"xs{l}")[c % G[l]] = total(f"xp{l}", l, f"xr{l}", f"xpr{l}").astype(bf)
                share_solution(l)
                wait_solution(l)
                for r in range(R):
                    at(f"fx{l}")[r] = at(f"xs{l}")[:, r].reshape(N, K[l])
            start_out(l)
        for l in (1, 2, 3):
            finish_out(l)
        for finish in sent:
            finish()

    return kernel, scratch


def fused_device(*blocks):
    plan = Plan(
        lax.axis_size("row"), lax.axis_size("col"),
        [block.shape for block in blocks[:4]], blocks[7].shape,
    )
    if not plan.fits():
        return per_device(*blocks)
    kernel, scratch = build_kernel(plan)
    vmem = pl.BlockSpec(memory_space=pltpu.VMEM)
    return pl.pallas_call(
        kernel,
        out_shape=tuple(jax.ShapeDtypeStruct(block.shape, block.dtype) for block in blocks[7:11]),
        in_specs=[vmem] * 14,
        out_specs=(vmem,) * 4,
        scratch_shapes=scratch,
        compiler_params=pltpu.CompilerParams(
            collective_id=0, has_side_effects=True, vmem_limit_bytes=56 * 2**20
        ),
    )(*blocks)


def solution(mesh):
    in_specs = (
        P("col", "row"),
        P("col", "row"),
        P("col", "row"),
        P("col", "row"),
        P("row", "col"),
        P("row", "col"),
        P("row", "col"),
        P("row", "col"),
        P("row", "col"),
        P("row", "col"),
        P("row", "col"),
        P(),
        P(),
        P(),
    )
    out_specs = (P("row", "col"), P("row", "col"), P("row", "col"), P("row", "col"))
    return jax.shard_map(
        fused_device, mesh=mesh, in_specs=in_specs, out_specs=out_specs, check_vma=False
    )
```

```python
import jax
import jax.numpy as jnp
from jax import lax
from jax.experimental import pallas as pl
from jax.experimental.pallas import tpu as pltpu
from jax.sharding import PartitionSpec as P


def swapped(value, axis, stride):
    mask = 2**stride
    pairs = [(source, source ^ mask) for source in range(lax.axis_size(axis))]
    return lax.ppermute(value, axis, pairs)


def route_tables(mapping, child_index, parent_sep, parent_upd, strips, row_index):
    positions = lax.dynamic_index_in_dim(mapping, child_index, 0, keepdims=False)
    sep_rows = parent_sep // strips
    in_separator = positions < parent_sep
    if parent_upd > 0:
        upd_rows = parent_upd // strips
        target = jnp.where(
            in_separator, positions // sep_rows, (positions - parent_sep) // upd_rows
        )
        offset = jnp.where(
            in_separator, positions % sep_rows, sep_rows + (positions - parent_sep) % upd_rows
        )
    else:
        target = positions // sep_rows
        offset = positions % sep_rows
    block_rows = positions.shape[0] // strips
    blocks = target.reshape(strips, block_rows)
    matches = (blocks[:, :, None] == jnp.arange(strips, dtype=jnp.int32)[None, None, :]).astype(
        jnp.int32
    )
    slot_of = jnp.sum((jnp.cumsum(matches, axis=1) - 1) * matches, axis=2).reshape(-1)
    block_len = sep_rows + parent_upd // strips
    capacity = 2 * positions.shape[0] // (strips * strips)
    source = jnp.arange(positions.shape[0], dtype=jnp.int32) // block_rows
    mine_here = target == row_index
    column_at = jnp.where(mine_here, slot_of, capacity)
    lookup = jnp.full((strips, capacity + 1), block_len, jnp.int32)
    lookup = lookup.at[source, column_at].set(jnp.where(mine_here, offset, block_len))[:, :capacity]
    local_target = lax.dynamic_slice_in_dim(target, row_index * block_rows, block_rows)
    local_slots = lax.dynamic_slice_in_dim(slot_of, row_index * block_rows, block_rows)
    return (local_target, local_slots, lookup, capacity, block_len)


def pack_rows(values, local_target, local_slots, strips, capacity):
    buffer = jnp.zeros((strips, capacity, values.shape[1]), values.dtype)
    return buffer.at[local_target, local_slots].set(values)


def unpack_rows(received, lookup, block_len):
    summed = jnp.zeros((block_len + 1, received.shape[2]), jnp.float32)
    return summed.at[lookup].add(received.astype(jnp.float32))[:block_len]


def spread(portion, depth_bits, pass_on, column):
    for bit_index in range(depth_bits):
        partner = pass_on(portion, bit_index)
        is_upper = column >> bit_index & 1 == 1
        portion = jnp.where(
            is_upper,
            jnp.concatenate([partner, portion], axis=-1),
            jnp.concatenate([portion, partner], axis=-1),
        )
    return portion


def shrink(entire, depth_bits, pass_on, column):
    for bit_index in reversed(range(depth_bits)):
        half_width = entire.shape[-1] // 2
        low_part = entire[..., :half_width]
        high_part = entire[..., half_width:]
        is_upper = column >> bit_index & 1 == 1
        kept_part = jnp.where(is_upper, high_part, low_part)
        sent_part = jnp.where(is_upper, low_part, high_part)
        entire = kept_part + pass_on(sent_part, bit_index)
    return entire


def per_device(
    inverse_top,
    inverse_one,
    inverse_two,
    inverse_leaf,
    coupling_one,
    coupling_two,
    coupling_leaf,
    rhs_top,
    rhs_one,
    rhs_two,
    rhs_leaf,
    parent_map_one,
    parent_map_two,
    parent_map_leaf,
):
    strips = lax.axis_size("row")
    col_count = lax.axis_size("col")
    row_here = lax.axis_index("row")
    column = lax.axis_index("col")
    inverses = [inverse_top, inverse_one, inverse_two, inverse_leaf]
    couplings = [None, coupling_one, coupling_two, coupling_leaf]
    right_sides = [rhs_top, rhs_one, rhs_two, rhs_leaf]
    parent_maps = [None, parent_map_one, parent_map_two, parent_map_leaf]
    orders = [inverse.shape[1] * strips for inverse in inverses]
    groups = [col_count >> tree_level for tree_level in range(4)]
    group_bits = [group_size.bit_length() - 1 for group_size in groups]
    pass_rhs = lambda values, bit_index: swapped(values, "col", bit_index)
    pass_update_sum = lambda values, bit_index: swapped(
        values.astype(jnp.bfloat16), "col", bit_index
    ).astype(values.dtype)
    pass_update_spread = lambda values, bit_index: swapped(values, "col", bit_index)
    pass_solution_sum = lambda values, bit_index: swapped(
        values.astype(jnp.bfloat16), "col", bit_index
    ).astype(values.dtype)
    pass_solution_spread = lambda values, bit_index: swapped(values, "col", bit_index)
    full_rhs = [
        spread(right_sides[tree_level], group_bits[tree_level], pass_rhs, column)
        for tree_level in range(4)
    ]
    own_routes = [None]
    for tree_level in range(1, 4):
        parent_order = orders[tree_level - 1]
        parent_update = parent_order if tree_level > 1 else 0
        front_here = column // groups[tree_level]
        own_routes.append(
            route_tables(
                parent_maps[tree_level], front_here, parent_order, parent_update, strips, row_here
            )
        )
    pivots = [None] * 4
    incoming = None
    for tree_level in (3, 2, 1, 0):
        sep_rows = inverses[tree_level].shape[1]
        if incoming is None:
            separator = full_rhs[tree_level]
            own_update = None
        else:
            separator = (full_rhs[tree_level].astype(jnp.float32) + incoming[:sep_rows]).astype(
                jnp.bfloat16
            )
            own_update = lax.optimization_barrier(incoming[sep_rows:].astype(jnp.bfloat16))
        partial_value = jnp.dot(inverses[tree_level], separator, preferred_element_type=jnp.float32)
        solved = lax.psum(partial_value.astype(jnp.bfloat16), "row")
        pivots[tree_level] = solved
        if tree_level > 0:
            coupled = jnp.dot(couplings[tree_level], solved, preferred_element_type=jnp.float32)
            reduced = shrink(coupled, group_bits[tree_level], pass_update_sum, column)
            if own_update is None:
                portion = (-reduced).astype(jnp.bfloat16)
            else:
                start_at = column % groups[tree_level] * reduced.shape[1]
                kept_rows = lax.dynamic_slice_in_dim(own_update, start_at, reduced.shape[1], 1)
                portion = (kept_rows.astype(jnp.float32) - reduced).astype(jnp.bfloat16)
            updated = spread(portion, group_bits[tree_level], pass_update_spread, column)
            own_target, own_slots, own_lookup, capacity, block_len = own_routes[tree_level]
            got_own = lax.all_to_all(
                pack_rows(updated, own_target, own_slots, strips, capacity),
                "row",
                split_axis=0,
                concat_axis=0,
                tiled=True,
            )
            own_part = unpack_rows(got_own, own_lookup, block_len)
            partner = swapped(own_part.astype(jnp.bfloat16), "col", group_bits[tree_level])
            incoming = own_part + partner.astype(jnp.float32)
    solutions = [None] * 4
    parent_solution = None
    parent_gathered = None
    for tree_level in range(4):
        solved = pivots[tree_level]
        gathered = None
        if tree_level == 0:
            residual = solved
        else:
            own_target, own_slots, own_lookup, capacity, block_len = own_routes[tree_level]
            pieces = [parent_solution]
            if parent_gathered is not None:
                pieces.append(parent_gathered)
            pieces.append(jnp.zeros((1, parent_solution.shape[1]), jnp.bfloat16))
            parent_rows = jnp.concatenate(pieces, axis=0)
            returned = lax.all_to_all(
                parent_rows[own_lookup], "row", split_axis=0, concat_axis=0, tiled=True
            )
            gathered = returned[own_target, own_slots]
            coupling_term = jnp.dot(
                couplings[tree_level].T, gathered, preferred_element_type=jnp.float32
            )
            residual = (
                solved.astype(jnp.float32)
                - lax.psum(coupling_term.astype(jnp.bfloat16), "row").astype(jnp.float32)
            ).astype(jnp.bfloat16)
        contribution = jnp.dot(inverses[tree_level].T, residual, preferred_element_type=jnp.float32)
        if tree_level == 0:
            summed = lax.psum(contribution.astype(jnp.bfloat16), "col")
            solution = summed
            rhs_width = solution.shape[1] // groups[0]
            solutions[0] = lax.dynamic_slice_in_dim(
                solution, column % groups[0] * rhs_width, rhs_width, 1
            )
        else:
            portion = shrink(
                contribution, group_bits[tree_level], pass_solution_sum, column
            ).astype(jnp.bfloat16)
            solutions[tree_level] = portion
            if tree_level < 3:
                solution = spread(portion, group_bits[tree_level], pass_solution_spread, column)
        parent_solution = solution
        parent_gathered = gathered
    return (solutions[0], solutions[1], solutions[2], solutions[3])


MESH = pl.DeviceIdType.MESH


def dot_nn(left, right):
    return lax.dot_general(left, right, (((1,), (0,)), ((), ())), preferred_element_type=jnp.float32)


def dot_nt(left, right):
    return lax.dot_general(left, right, (((1,), (1,)), ((), ())), preferred_element_type=jnp.float32)


def eye(size):
    rows = lax.broadcasted_iota(jnp.int32, (size, size), 0)
    columns = lax.broadcasted_iota(jnp.int32, (size, size), 1)
    return jnp.where(rows == columns, 1.0, 0.0).astype(jnp.bfloat16)


def flipped(value, mask):
    result = value
    bit = 1
    while bit <= mask:
        if mask & bit:
            result = result + bit * (1 - 2 * ((value // bit) % 2))
        bit *= 2
    return result


class Plan:
    def __init__(self, rows, cols, inverse_shapes, rhs_top_shape):
        self.rows, self.cols = rows, cols
        self.strip = [shape[1] for shape in inverse_shapes]
        self.order = [shape[1] * rows for shape in inverse_shapes]
        self.local = [shape[0] for shape in inverse_shapes]
        self.group = [cols >> level for level in range(4)]
        self.columns = rhs_top_shape[1] * cols
        self.width = [self.columns // group if group else 0 for group in self.group]
        self.mine = self.columns // rows

    def total(self, level):
        return self.order[level] * (2 if level else 1)

    def fits(self):
        table = sum(
            2 * self.total(level) * self.order[level + 1] * 2 for level in range(3)
        )
        if self.rows < 3 or self.group[3] != 1 or self.mine * self.rows != self.columns or table > 24 * 2**20:
            return False
        for level in range(4):
            if self.strip[level] % 16 or self.order[level] % 128 or self.width[level] % 16:
                return False
            if max(self.width[level], self.mine) % min(self.width[level], self.mine):
                return False
        for level in (1, 2):
            if self.mine % (16 * self.group[level]):
                return False
        return self.order[0] % (128 * self.group[0]) == 0 and self.group[0] % self.rows == 0


def narrow(size):
    return size < 128


def build_kernel(plan):
    R, CC, N = plan.rows, plan.cols, plan.mine
    S, K, L, G, W = plan.order, plan.strip, plan.local, plan.group, plan.width
    bf = jnp.bfloat16
    scratch, names = [], {}

    def ref(name, shape, dtype=bf):
        names[name] = len(scratch)
        scratch.append(pltpu.VMEM(shape, dtype))

    def sems(name, shape):
        names[name] = len(scratch)
        scratch.append(pltpu.SemaphoreType.DMA(shape))

    for l in range(4):
        n_dest = max(1, W[l] // N)
        n_part = max(1, N // W[l])
        ref(f"Z{l}", (R, K[l], L[l]) if narrow(K[l]) else (R, L[l], K[l]))
        sems(f"Zs{l}", (2, R))
        sems(f"Zr{l}", (2, R))
        if l:
            ref(f"C{l}", (S[l], L[l]))
            sems(f"Cs{l}", (2, R))
            sems(f"Cr{l}", (2, R))
        ref(f"bT{l}", (W[l], K[l]))
        ref(f"B{l}", (R, N, K[l]))
        sems(f"Bs{l}", (n_dest,))
        sems(f"Br{l}", (R,))
        sems(f"Ds{l}", (G[l],))
        sems(f"Dr{l}", (n_part,))
        ref(f"y{l}", (N, L[l]))
        ref(f"fx{l}", (R, N, K[l]))
        ref(f"oT{l}", (W[l], K[l]))
        sems(f"Os{l}", (R,))
        sems(f"Or{l}", (n_dest,))
        if l < 3:
            ref(f"hot{l}", (2, plan.total(l), S[l + 1]))
            if l:
                shape = (G[l], R, N // G[l], K[l])
                ref(f"xp{l}", shape)
                ref(f"xr{l}", shape)
                ref(f"xs{l}", shape)
            else:
                shape = (G[0], N, S[0] // G[0])
                ref("xp0", shape)
                ref("xr0", shape)
                ref("xs0", shape)
            for tag in ("xps", "xpr", "xss", "xsr"):
                sems(f"{tag}{l}", (G[l],))
        if l:
            shape = (G[l], N // G[l], S[l])
            ref(f"u{l}", (2,) + shape)
            sems(f"us{l}", (2 * G[l],))
            sems(f"ur{l}", (2 * G[l],))
            ref(f"v{l}", (N, S[l]))
            if G[l] > 1:
                ref(f"H{l}", shape)
                ref(f"up{l}", shape)
                ref(f"ut{l}", shape)
                sems(f"ups{l}", (G[l],))
                sems(f"upr{l}", (G[l],))

    def kernel(*refs):
        inverse = refs[0:4]
        coupling = (None,) + tuple(refs[4:7])
        rhs = refs[7:11]
        maps = (None,) + tuple(refs[11:14])
        outs = refs[14:18]
        held = refs[18:]
        at = lambda name: held[names[name]]
        z = lax.axis_index("row")
        c = lax.axis_index("col")
        sent = []

        def remote(src, dst, ssem, rsem, z_to, c_to):
            return pltpu.make_async_remote_copy(
                src_ref=src, dst_ref=dst, send_sem=ssem, recv_sem=rsem,
                device_id=(z_to, c_to), device_id_type=MESH,
            )

        def send(src, dst, ssem, rsem, z_to, c_to):
            copy = remote(src, dst, ssem, rsem, z_to, c_to)
            copy.start()
            sent.append(copy.wait_send)

        def send_or_copy(src, dst, ssem, rsem, z_to, c_to, here):
            @pl.when(here)
            def _():
                pltpu.make_async_copy(src, dst, rsem).start()

            @pl.when(jnp.logical_not(here))
            def _():
                remote(src, dst, ssem, rsem, z_to, c_to).start()

            def finish():
                @pl.when(jnp.logical_not(here))
                def _():
                    remote(src, dst, ssem, rsem, z_to, c_to).wait_send()

            sent.append(finish)

        def arrived(dst, rsem):
            pltpu.make_async_copy(dst, dst, rsem).wait()

        barrier = pltpu.get_barrier_semaphore()
        for d in range(1, R):
            pl.semaphore_signal(
                barrier, inc=1, device_id=((z + d) % R, c), device_id_type=MESH
            )
        for m in range(1, CC):
            pl.semaphore_signal(
                barrier, inc=1, device_id=(z, flipped(c, m)), device_id_type=MESH
            )
        turned = []
        for l in range(4):
            if narrow(W[l]):
                turned.append(rhs[l])
            else:
                at(f"bT{l}")[...] = dot_nt(eye(W[l]), rhs[l][...]).astype(bf)
                turned.append(at(f"bT{l}"))
        pl.semaphore_wait(barrier, R + CC - 2)

        def start_rhs(l):
            q = c % G[l]
            n_dest, n_part = max(1, W[l] // N), max(1, N // W[l])
            for i in range(n_dest):
                if W[l] >= N:
                    z_to = q * n_dest + i
                    src = turned[l].at[pl.ds(i * N, N)]
                    dst = at(f"B{l}").at[z]
                else:
                    z_to = q // n_part
                    src = turned[l]
                    low = pl.multiple_of((q % n_part) * W[l], W[l])
                    dst = at(f"B{l}").at[z, pl.ds(low, W[l])]
                ssem, rsem = at(f"Bs{l}").at[i], at(f"Br{l}").at[z]
                send_or_copy(src, dst, ssem, rsem, z_to, c, z_to == z)

        def rhs_part(l, part):
            if W[l] >= N:
                return at(f"B{l}")
            return at(f"B{l}").at[:, pl.ds(pl.multiple_of(part * W[l], W[l]), W[l])]

        def spread_rhs(l):
            q = c % G[l]
            n_dest, n_part = max(1, W[l] // N), max(1, N // W[l])
            holds = z // n_dest == q // n_part
            part = q % n_part
            here = rhs_part(l, part)

            def copy_to(m):
                return remote(
                    here, here, at(f"Ds{l}").at[m], at(f"Dr{l}").at[part], z, flipped(c, m)
                )

            @pl.when(holds)
            def _():
                for r in range(R):
                    block = at(f"B{l}").at[r]
                    if n_part > 1:
                        low = pl.multiple_of(part * W[l], W[l])
                        block = at(f"B{l}").at[r, pl.ds(low, W[l])]
                    arrived(block, at(f"Br{l}").at[r])
                for m in range(1, G[l]):
                    copy_to(m).start()

            def finish():
                @pl.when(holds)
                def _():
                    for m in range(1, G[l]):
                        copy_to(m).wait_send()

            sent.append(finish)

        def wait_rhs(l):
            q = c % G[l]
            n_dest, n_part = max(1, W[l] // N), max(1, N // W[l])
            for part in range(n_part):
                @pl.when(z // n_dest * n_part + part != q)
                def _():
                    arrived(rhs_part(l, part), at(f"Dr{l}").at[part])

        def z_block(l, index):
            return at(f"Z{l}").at[index]

        def c_block(l, index):
            return at(f"C{l}").at[pl.ds(pl.multiple_of(index * K[l], 16), K[l])]

        kinds = {"Z": (inverse, z_block), "C": (coupling, c_block)}

        def start_line(kind, l):
            source, block = kinds[kind]
            src, dst = source[l], block(l, z)
            pltpu.make_async_copy(src, dst, at(f"{kind}r{l}").at[0, 0]).start()
            for way, step in ((0, 1), (1, -1)):
                go_on(kind, l, way, step, 0, src, z)

        def go_on(kind, l, way, step, d, src, origin):
            open_end = jnp.logical_and(z + step >= 0, z + step < R)
            begun = jnp.logical_and(z - d * step >= 0, z - d * step < R)
            ready = jnp.logical_and(open_end, begun)
            dst = kinds[kind][1](l, origin)

            def copy():
                return remote(
                    src, dst, at(f"{kind}s{l}").at[way, d], at(f"{kind}r{l}").at[way, d + 1],
                    (z + step + R) % R, c,
                )

            @pl.when(ready)
            def _():
                copy().start()

            def finish():
                @pl.when(ready)
                def _():
                    copy().wait_send()

            sent.append(finish)

        def pass_line(kind, l, d):
            for way, step in ((0, 1), (1, -1)):
                origin = (z - d * step + R) % R
                block = kinds[kind][1](l, origin)
                begun = jnp.logical_and(z - d * step >= 0, z - d * step < R)

                @pl.when(begun)
                def _():
                    arrived(block, at(f"{kind}r{l}").at[way, d])

                if d < R - 1:
                    go_on(kind, l, way, step, d, block, origin)

        def pass_both(l, d):
            pass_line("Z", l, d)
            if l:
                pass_line("C", l, d)

        def own_line(kind, l):
            arrived(kinds[kind][1](l, z), at(f"{kind}r{l}").at[0, 0])

        def scatter(name, l, landed, ssem, rsem):
            q = c % G[l]
            for m in range(1, G[l]):
                send(
                    at(name).at[flipped(q, m)], at(landed).at[m],
                    at(ssem).at[m], at(rsem).at[m], z, flipped(c, m),
                )

        def total(name, l, landed, rsem):
            value = at(name)[c % G[l]].astype(jnp.float32)
            for m in range(1, G[l]):
                arrived(at(landed).at[m], at(rsem).at[m])
                value = value + at(landed)[m].astype(jnp.float32)
            return value

        def share_solution(l):
            q = c % G[l]
            here = at(f"xs{l}").at[q]
            for m in range(1, G[l]):
                send(here, here, at(f"xss{l}").at[m], at(f"xsr{l}").at[m], z, flipped(c, m))

        def wait_solution(l):
            q = c % G[l]
            for m in range(1, G[l]):
                arrived(at(f"xs{l}").at[flipped(q, m)], at(f"xsr{l}").at[m])

        def share_update(l):
            child, q = (c // G[l]) % 2, c % G[l]
            here = at(f"u{l}").at[child, q]
            for m in range(1, 2 * G[l]):
                send(here, here, at(f"us{l}").at[m], at(f"ur{l}").at[m], z, flipped(c, m))

        def wait_update(l):
            for m in range(1, 2 * G[l]):
                other = flipped(c, m)
                arrived(
                    at(f"u{l}").at[(other // G[l]) % 2, other % G[l]], at(f"ur{l}").at[m]
                )

        def make_table(l):
            front = c // G[l]
            step = K[l]
            for child in range(2):
                row = maps[l + 1][pl.ds(2 * front + child, 1), :]

                def body(i, carry):
                    start = pl.multiple_of(i * step, 16)
                    at_row = lax.broadcasted_iota(jnp.int32, (step, S[l + 1]), 0) + start
                    at(f"hot{l}")[child, pl.ds(start, step), :] = jnp.where(
                        at_row == row, 1.0, 0.0
                    ).astype(bf)
                    return carry

                lax.fori_loop(0, plan.total(l) // step, body, 0)

        def start_out(l):
            q = c % G[l]
            n_dest, n_part = max(1, W[l] // N), max(1, N // W[l])
            if W[l] >= N:
                holds = z // n_dest == q
                index = z % n_dest
                dst = at(f"oT{l}").at[pl.ds(pl.multiple_of(index * N, N), N)]
            else:
                holds = q // n_part == z
                index = 0
                dst = at(f"oT{l}")

            def piece(r):
                if W[l] >= N:
                    return at(f"fx{l}").at[r]
                low = pl.multiple_of((q % n_part) * W[l], W[l])
                return at(f"fx{l}").at[r, pl.ds(low, W[l])]

            def copy_to(d):
                r = (z + d) % R
                return remote(
                    piece(r), dst, at(f"Os{l}").at[d], at(f"Or{l}").at[index], r, c
                )

            @pl.when(holds)
            def _():
                pltpu.make_async_copy(piece(z), dst, at(f"Or{l}").at[index]).start()
                for d in range(1, R):
                    copy_to(d).start()

            def finish():
                @pl.when(holds)
                def _():
                    for d in range(1, R):
                        copy_to(d).wait_send()

            sent.append(finish)

        def finish_out(l):
            if W[l] >= N:
                for i in range(W[l] // N):
                    arrived(at(f"oT{l}").at[pl.ds(i * N, N)], at(f"Or{l}").at[i])
            else:
                arrived(at(f"oT{l}"), at(f"Or{l}").at[0])
            if narrow(W[l]):
                outs[l][...] = at(f"oT{l}")[...]
            else:
                outs[l][...] = dot_nt(eye(K[l]), at(f"oT{l}")[...]).astype(bf)

        def pivot(l, blocks):
            product = dot_nn if narrow(K[l]) else dot_nt
            value = product(blocks[0], at(f"Z{l}")[0])
            for r in range(1, R):
                value = value + product(blocks[r], at(f"Z{l}")[r])
            at(f"y{l}")[...] = value.astype(bf)

        start_line("Z", 3)
        start_line("C", 3)
        start_rhs(3)
        start_line("Z", 2)
        for l in (2, 1, 0):
            start_rhs(l)
        make_table(2)
        pass_both(3, 1)
        start_line("C", 2)
        for d in range(2, R):
            pass_both(3, d)
            if d == 2:
                pass_both(2, 1)
                start_line("Z", 1)
        for l in (2, 1, 0):
            spread_rhs(l)
        spread_rhs(3)
        own_line("Z", 3)
        pivot(3, [at("B3")[r] for r in range(R)])
        own_line("C", 3)
        at("u3")[(c // G[3]) % 2, 0] = (-dot_nt(at("y3")[...], at("C3")[...])).astype(bf)
        share_update(3)
        pass_both(2, 2)
        start_line("C", 1)
        pass_line("Z", 1, 1)
        make_table(1)
        for d in range(3, R):
            pass_both(2, d)

        for l in (2, 1, 0):
            wait_update(l + 1)
            pair = [at(f"u{l + 1}")[child].reshape(N, S[l + 1]) for child in range(2)]

            def assembled(low, size):
                value = dot_nt(pair[0], at(f"hot{l}")[0, low:low + size, :])
                return value + dot_nt(pair[1], at(f"hot{l}")[1, low:low + size, :])

            wait_rhs(l)
            blocks = [
                (at(f"B{l}")[r].astype(jnp.float32) + assembled(r * K[l], K[l])).astype(bf)
                for r in range(R)
            ]
            if l == 1:
                for d in range(3, R):
                    pass_both(1, d)
                pass_line("Z", 0, 2)
            if l == 0:
                for d in range(3, R):
                    pass_line("Z", 0, d)
            own_line("Z", l)
            pivot(l, blocks)
            if l:
                own_line("C", l)
                share = (G[l], N // G[l], S[l])
                at(f"up{l}")[...] = (
                    dot_nt(at(f"y{l}")[...], at(f"C{l}")[...]).astype(bf).reshape(share)
                )
                scatter(f"up{l}", l, f"ut{l}", f"ups{l}", f"upr{l}")
                if l == 2:
                    pass_line("C", 1, 1)
                    start_line("Z", 0)
                    pass_line("Z", 1, 2)
                    make_table(0)
                    pass_line("C", 1, 2)
                    pass_line("Z", 0, 1)
                at(f"H{l}")[...] = assembled(S[l], S[l]).astype(bf).reshape(share)
                reduced = total(f"up{l}", l, f"ut{l}", f"upr{l}")
                q = c % G[l]
                at(f"u{l}")[(c // G[l]) % 2, q] = (
                    at(f"H{l}")[q].astype(jnp.float32) - reduced
                ).astype(bf)
                share_update(l)

        per = G[0] // R
        lanes = S[0] // G[0]
        for r in range(R):
            product = dot_nt if narrow(K[0]) else dot_nn
            value = product(at("y0")[...], at("Z0")[r]).astype(bf)
            for i in range(per):
                at("xp0")[r * per + i] = value[:, i * lanes:(i + 1) * lanes]
        scatter("xp0", 0, "xr0", "xps0", "xpr0")
        at("xs0")[c % G[0]] = total("xp0", 0, "xr0", "xpr0").astype(bf)
        share_solution(0)
        wait_solution(0)
        for r in range(R):
            for i in range(per):
                at("fx0")[r, :, i * lanes:(i + 1) * lanes] = at("xs0")[r * per + i]
        start_out(0)

        for l in (1, 2, 3):
            child = (c // G[l]) % 2
            gathered = dot_nn(at(f"fx{l - 1}")[0], at(f"hot{l - 1}")[child, 0:K[l - 1], :])
            for r in range(1, R):
                gathered = gathered + dot_nn(
                    at(f"fx{l - 1}")[r],
                    at(f"hot{l - 1}")[child, r * K[l - 1]:(r + 1) * K[l - 1], :],
                )
            if l > 1:
                gathered = gathered + dot_nn(
                    at(f"v{l - 1}")[...], at(f"hot{l - 1}")[child, S[l - 1]:, :]
                )
            at(f"v{l}")[...] = gathered.astype(bf)
            residual = (
                at(f"y{l}")[...].astype(jnp.float32)
                - dot_nn(at(f"v{l}")[...], at(f"C{l}")[...])
            ).astype(bf)
            for r in range(R):
                product = dot_nt if narrow(K[l]) else dot_nn
                value = product(residual, at(f"Z{l}")[r]).astype(bf)
                if G[l] > 1:
                    at(f"xp{l}")[:, r] = value.reshape(G[l], N // G[l], K[l])
                else:
                    at(f"fx{l}")[r] = value
            if G[l] > 1:
                scatter(f"xp{l}", l, f"xr{l}", f"xps{l}", f"xpr{l}")
                if l == 1:
                    finish_out(0)
                at(f"xs{l}")[c % G[l]] = total(f"xp{l}", l, f"xr{l}", f"xpr{l}").astype(bf)
                share_solution(l)
                wait_solution(l)
                for r in range(R):
                    at(f"fx{l}")[r] = at(f"xs{l}")[:, r].reshape(N, K[l])
            start_out(l)
        for l in (1, 2, 3):
            finish_out(l)
        for finish in sent:
            finish()

    return kernel, scratch


def fused_device(*blocks):
    plan = Plan(
        lax.axis_size("row"), lax.axis_size("col"),
        [block.shape for block in blocks[:4]], blocks[7].shape,
    )
    if not plan.fits():
        return per_device(*blocks)
    kernel, scratch = build_kernel(plan)
    blocks = list(blocks)
    for at in (0, 1, 2, 3, 7, 8, 9, 10):
        if narrow(blocks[at].shape[1]):
            blocks[at] = blocks[at].T
    vmem = pl.BlockSpec(memory_space=pltpu.VMEM)
    solved = pl.pallas_call(
        kernel,
        out_shape=tuple(jax.ShapeDtypeStruct(block.shape, block.dtype) for block in blocks[7:11]),
        in_specs=[vmem] * 14,
        out_specs=(vmem,) * 4,
        scratch_shapes=scratch,
        compiler_params=pltpu.CompilerParams(
            collective_id=0, has_side_effects=True, vmem_limit_bytes=56 * 2**20
        ),
    )(*blocks)
    return tuple(
        block.T if narrow(width) else block for block, width in zip(solved, plan.width)
    )


def solution(mesh):
    in_specs = (
        P("col", "row"),
        P("col", "row"),
        P("col", "row"),
        P("col", "row"),
        P("row", "col"),
        P("row", "col"),
        P("row", "col"),
        P("row", "col"),
        P("row", "col"),
        P("row", "col"),
        P("row", "col"),
        P(),
        P(),
        P(),
    )
    out_specs = (P("row", "col"), P("row", "col"), P("row", "col"), P("row", "col"))
    return jax.shard_map(
        fused_device, mesh=mesh, in_specs=in_specs, out_specs=out_specs, check_vma=False
    )
```

```python
import jax
import jax.numpy as jnp
from jax import lax
from jax.experimental import pallas as pl
from jax.experimental.pallas import tpu as pltpu
from jax.sharding import PartitionSpec as P


def swapped(value, axis, stride):
    mask = 2**stride
    pairs = [(source, source ^ mask) for source in range(lax.axis_size(axis))]
    return lax.ppermute(value, axis, pairs)


def route_tables(mapping, child_index, parent_sep, parent_upd, strips, row_index):
    positions = lax.dynamic_index_in_dim(mapping, child_index, 0, keepdims=False)
    sep_rows = parent_sep // strips
    in_separator = positions < parent_sep
    if parent_upd > 0:
        upd_rows = parent_upd // strips
        target = jnp.where(
            in_separator, positions // sep_rows, (positions - parent_sep) // upd_rows
        )
        offset = jnp.where(
            in_separator, positions % sep_rows, sep_rows + (positions - parent_sep) % upd_rows
        )
    else:
        target = positions // sep_rows
        offset = positions % sep_rows
    block_rows = positions.shape[0] // strips
    blocks = target.reshape(strips, block_rows)
    matches = (blocks[:, :, None] == jnp.arange(strips, dtype=jnp.int32)[None, None, :]).astype(
        jnp.int32
    )
    slot_of = jnp.sum((jnp.cumsum(matches, axis=1) - 1) * matches, axis=2).reshape(-1)
    block_len = sep_rows + parent_upd // strips
    capacity = 2 * positions.shape[0] // (strips * strips)
    source = jnp.arange(positions.shape[0], dtype=jnp.int32) // block_rows
    mine_here = target == row_index
    column_at = jnp.where(mine_here, slot_of, capacity)
    lookup = jnp.full((strips, capacity + 1), block_len, jnp.int32)
    lookup = lookup.at[source, column_at].set(jnp.where(mine_here, offset, block_len))[:, :capacity]
    local_target = lax.dynamic_slice_in_dim(target, row_index * block_rows, block_rows)
    local_slots = lax.dynamic_slice_in_dim(slot_of, row_index * block_rows, block_rows)
    return (local_target, local_slots, lookup, capacity, block_len)


def pack_rows(values, local_target, local_slots, strips, capacity):
    buffer = jnp.zeros((strips, capacity, values.shape[1]), values.dtype)
    return buffer.at[local_target, local_slots].set(values)


def unpack_rows(received, lookup, block_len):
    summed = jnp.zeros((block_len + 1, received.shape[2]), jnp.float32)
    return summed.at[lookup].add(received.astype(jnp.float32))[:block_len]


def spread(portion, depth_bits, pass_on, column):
    for bit_index in range(depth_bits):
        partner = pass_on(portion, bit_index)
        is_upper = column >> bit_index & 1 == 1
        portion = jnp.where(
            is_upper,
            jnp.concatenate([partner, portion], axis=-1),
            jnp.concatenate([portion, partner], axis=-1),
        )
    return portion


def shrink(entire, depth_bits, pass_on, column):
    for bit_index in reversed(range(depth_bits)):
        half_width = entire.shape[-1] // 2
        low_part = entire[..., :half_width]
        high_part = entire[..., half_width:]
        is_upper = column >> bit_index & 1 == 1
        kept_part = jnp.where(is_upper, high_part, low_part)
        sent_part = jnp.where(is_upper, low_part, high_part)
        entire = kept_part + pass_on(sent_part, bit_index)
    return entire


def per_device(
    inverse_top,
    inverse_one,
    inverse_two,
    inverse_leaf,
    coupling_one,
    coupling_two,
    coupling_leaf,
    rhs_top,
    rhs_one,
    rhs_two,
    rhs_leaf,
    parent_map_one,
    parent_map_two,
    parent_map_leaf,
):
    strips = lax.axis_size("row")
    col_count = lax.axis_size("col")
    row_here = lax.axis_index("row")
    column = lax.axis_index("col")
    inverses = [inverse_top, inverse_one, inverse_two, inverse_leaf]
    couplings = [None, coupling_one, coupling_two, coupling_leaf]
    right_sides = [rhs_top, rhs_one, rhs_two, rhs_leaf]
    parent_maps = [None, parent_map_one, parent_map_two, parent_map_leaf]
    orders = [inverse.shape[1] * strips for inverse in inverses]
    groups = [col_count >> tree_level for tree_level in range(4)]
    group_bits = [group_size.bit_length() - 1 for group_size in groups]
    pass_rhs = lambda values, bit_index: swapped(values, "col", bit_index)
    pass_update_sum = lambda values, bit_index: swapped(
        values.astype(jnp.bfloat16), "col", bit_index
    ).astype(values.dtype)
    pass_update_spread = lambda values, bit_index: swapped(values, "col", bit_index)
    pass_solution_sum = lambda values, bit_index: swapped(
        values.astype(jnp.bfloat16), "col", bit_index
    ).astype(values.dtype)
    pass_solution_spread = lambda values, bit_index: swapped(values, "col", bit_index)
    full_rhs = [
        spread(right_sides[tree_level], group_bits[tree_level], pass_rhs, column)
        for tree_level in range(4)
    ]
    own_routes = [None]
    for tree_level in range(1, 4):
        parent_order = orders[tree_level - 1]
        parent_update = parent_order if tree_level > 1 else 0
        front_here = column // groups[tree_level]
        own_routes.append(
            route_tables(
                parent_maps[tree_level], front_here, parent_order, parent_update, strips, row_here
            )
        )
    pivots = [None] * 4
    incoming = None
    for tree_level in (3, 2, 1, 0):
        sep_rows = inverses[tree_level].shape[1]
        if incoming is None:
            separator = full_rhs[tree_level]
            own_update = None
        else:
            separator = (full_rhs[tree_level].astype(jnp.float32) + incoming[:sep_rows]).astype(
                jnp.bfloat16
            )
            own_update = lax.optimization_barrier(incoming[sep_rows:].astype(jnp.bfloat16))
        partial_value = jnp.dot(inverses[tree_level], separator, preferred_element_type=jnp.float32)
        solved = lax.psum(partial_value.astype(jnp.bfloat16), "row")
        pivots[tree_level] = solved
        if tree_level > 0:
            coupled = jnp.dot(couplings[tree_level], solved, preferred_element_type=jnp.float32)
            reduced = shrink(coupled, group_bits[tree_level], pass_update_sum, column)
            if own_update is None:
                portion = (-reduced).astype(jnp.bfloat16)
            else:
                start_at = column % groups[tree_level] * reduced.shape[1]
                kept_rows = lax.dynamic_slice_in_dim(own_update, start_at, reduced.shape[1], 1)
                portion = (kept_rows.astype(jnp.float32) - reduced).astype(jnp.bfloat16)
            updated = spread(portion, group_bits[tree_level], pass_update_spread, column)
            own_target, own_slots, own_lookup, capacity, block_len = own_routes[tree_level]
            got_own = lax.all_to_all(
                pack_rows(updated, own_target, own_slots, strips, capacity),
                "row",
                split_axis=0,
                concat_axis=0,
                tiled=True,
            )
            own_part = unpack_rows(got_own, own_lookup, block_len)
            partner = swapped(own_part.astype(jnp.bfloat16), "col", group_bits[tree_level])
            incoming = own_part + partner.astype(jnp.float32)
    solutions = [None] * 4
    parent_solution = None
    parent_gathered = None
    for tree_level in range(4):
        solved = pivots[tree_level]
        gathered = None
        if tree_level == 0:
            residual = solved
        else:
            own_target, own_slots, own_lookup, capacity, block_len = own_routes[tree_level]
            pieces = [parent_solution]
            if parent_gathered is not None:
                pieces.append(parent_gathered)
            pieces.append(jnp.zeros((1, parent_solution.shape[1]), jnp.bfloat16))
            parent_rows = jnp.concatenate(pieces, axis=0)
            returned = lax.all_to_all(
                parent_rows[own_lookup], "row", split_axis=0, concat_axis=0, tiled=True
            )
            gathered = returned[own_target, own_slots]
            coupling_term = jnp.dot(
                couplings[tree_level].T, gathered, preferred_element_type=jnp.float32
            )
            residual = (
                solved.astype(jnp.float32)
                - lax.psum(coupling_term.astype(jnp.bfloat16), "row").astype(jnp.float32)
            ).astype(jnp.bfloat16)
        contribution = jnp.dot(inverses[tree_level].T, residual, preferred_element_type=jnp.float32)
        if tree_level == 0:
            summed = lax.psum(contribution.astype(jnp.bfloat16), "col")
            solution = summed
            rhs_width = solution.shape[1] // groups[0]
            solutions[0] = lax.dynamic_slice_in_dim(
                solution, column % groups[0] * rhs_width, rhs_width, 1
            )
        else:
            portion = shrink(
                contribution, group_bits[tree_level], pass_solution_sum, column
            ).astype(jnp.bfloat16)
            solutions[tree_level] = portion
            if tree_level < 3:
                solution = spread(portion, group_bits[tree_level], pass_solution_spread, column)
        parent_solution = solution
        parent_gathered = gathered
    return (solutions[0], solutions[1], solutions[2], solutions[3])


MESH = pl.DeviceIdType.MESH


def dot_nn(left, right):
    return lax.dot_general(left, right, (((1,), (0,)), ((), ())), preferred_element_type=jnp.float32)


def dot_nt(left, right):
    return lax.dot_general(left, right, (((1,), (1,)), ((), ())), preferred_element_type=jnp.float32)


def eye(size):
    rows = lax.broadcasted_iota(jnp.int32, (size, size), 0)
    columns = lax.broadcasted_iota(jnp.int32, (size, size), 1)
    return jnp.where(rows == columns, 1.0, 0.0).astype(jnp.bfloat16)


def flipped(value, mask):
    result = value
    bit = 1
    while bit <= mask:
        if mask & bit:
            result = result + bit * (1 - 2 * ((value // bit) % 2))
        bit *= 2
    return result


class Plan:
    def __init__(self, rows, cols, inverse_shapes, rhs_top_shape):
        self.rows, self.cols = rows, cols
        self.strip = [shape[1] for shape in inverse_shapes]
        self.order = [shape[1] * rows for shape in inverse_shapes]
        self.local = [shape[0] for shape in inverse_shapes]
        self.group = [cols >> level for level in range(4)]
        self.columns = rhs_top_shape[1] * cols
        self.width = [self.columns // group if group else 0 for group in self.group]
        self.mine = self.columns // rows

    def total(self, level):
        return self.order[level] * (2 if level else 1)

    def fits(self):
        table = sum(
            2 * self.total(level) * self.order[level + 1] * 2 for level in range(3)
        )
        if self.rows < 3 or self.group[3] != 1 or self.mine * self.rows != self.columns or table > 24 * 2**20:
            return False
        for level in range(4):
            if self.strip[level] % 16 or self.order[level] % 128 or self.width[level] % 16:
                return False
            if max(self.width[level], self.mine) % min(self.width[level], self.mine):
                return False
        for level in (1, 2):
            if self.mine % (16 * self.group[level]):
                return False
        return self.order[0] % (128 * self.group[0]) == 0 and self.group[0] % self.rows == 0


def narrow(size):
    return size < 128


def build_kernel(plan):
    R, CC, N = plan.rows, plan.cols, plan.mine
    S, K, L, G, W = plan.order, plan.strip, plan.local, plan.group, plan.width
    bf = jnp.bfloat16
    scratch, names = [], {}

    def ref(name, shape, dtype=bf):
        names[name] = len(scratch)
        scratch.append(pltpu.VMEM(shape, dtype))

    def sems(name, shape):
        names[name] = len(scratch)
        scratch.append(pltpu.SemaphoreType.DMA(shape))

    for l in range(4):
        n_dest = max(1, W[l] // N)
        n_part = max(1, N // W[l])
        ref(f"Z{l}", (R, K[l], L[l]) if narrow(K[l]) else (R, L[l], K[l]))
        sems(f"Zs{l}", (2, R))
        sems(f"Zr{l}", (2, R))
        if l:
            ref(f"C{l}", (S[l], L[l]))
            sems(f"Cs{l}", (2, R))
            sems(f"Cr{l}", (2, R))
        ref(f"bT{l}", (W[l], K[l]))
        ref(f"B{l}", (R, N, K[l]))
        sems(f"Bs{l}", (n_dest,))
        sems(f"Br{l}", (R,))
        sems(f"Ds{l}", (G[l],))
        sems(f"Dr{l}", (n_part,))
        ref(f"y{l}", (N, L[l]))
        ref(f"fx{l}", (R, N, K[l]))
        ref(f"oT{l}", (W[l], K[l]))
        sems(f"Os{l}", (R,))
        sems(f"Or{l}", (n_dest,))
        if l < 3:
            ref(f"hot{l}", (2, plan.total(l), S[l + 1]))
            if l:
                shape = (G[l], R, N // G[l], K[l])
                ref(f"xp{l}", shape)
                ref(f"xr{l}", shape)
                ref(f"xs{l}", shape)
            else:
                shape = (G[0], N, S[0] // G[0])
                ref("xp0", shape)
                ref("xr0", shape)
                ref("xs0", shape)
            for tag in ("xps", "xpr", "xss", "xsr"):
                sems(f"{tag}{l}", (G[l],))
        if l:
            shape = (G[l], N // G[l], S[l])
            ref(f"u{l}", (2,) + shape)
            sems(f"us{l}", (2 * G[l],))
            sems(f"ur{l}", (2 * G[l],))
            ref(f"v{l}", (N, S[l]))
            if G[l] > 1:
                ref(f"H{l}", shape)
                ref(f"up{l}", shape)
                ref(f"ut{l}", shape)
                sems(f"ups{l}", (G[l],))
                sems(f"upr{l}", (G[l],))

    def kernel(*refs):
        inverse = refs[0:4]
        coupling = (None,) + tuple(refs[4:7])
        rhs = refs[7:11]
        maps = (None,) + tuple(refs[11:14])
        outs = refs[14:18]
        held = refs[18:]
        at = lambda name: held[names[name]]
        z = lax.axis_index("row")
        c = lax.axis_index("col")
        sent = []

        def remote(src, dst, ssem, rsem, z_to, c_to):
            return pltpu.make_async_remote_copy(
                src_ref=src, dst_ref=dst, send_sem=ssem, recv_sem=rsem,
                device_id=(z_to, c_to), device_id_type=MESH,
            )

        def send(src, dst, ssem, rsem, z_to, c_to):
            copy = remote(src, dst, ssem, rsem, z_to, c_to)
            copy.start()
            sent.append(copy.wait_send)

        def send_or_copy(src, dst, ssem, rsem, z_to, c_to, here):
            @pl.when(here)
            def _():
                pltpu.make_async_copy(src, dst, rsem).start()

            @pl.when(jnp.logical_not(here))
            def _():
                remote(src, dst, ssem, rsem, z_to, c_to).start()

            def finish():
                @pl.when(jnp.logical_not(here))
                def _():
                    remote(src, dst, ssem, rsem, z_to, c_to).wait_send()

            sent.append(finish)

        def arrived(dst, rsem):
            pltpu.make_async_copy(dst, dst, rsem).wait()

        barrier = pltpu.get_barrier_semaphore()
        for d in range(1, R):
            pl.semaphore_signal(
                barrier, inc=1, device_id=((z + d) % R, c), device_id_type=MESH
            )
        for m in range(1, CC):
            pl.semaphore_signal(
                barrier, inc=1, device_id=(z, flipped(c, m)), device_id_type=MESH
            )
        turned = []
        for l in range(4):
            if narrow(W[l]):
                turned.append(rhs[l])
            else:
                at(f"bT{l}")[...] = dot_nt(eye(W[l]), rhs[l][...]).astype(bf)
                turned.append(at(f"bT{l}"))
        pl.semaphore_wait(barrier, R + CC - 2)

        def start_rhs(l):
            q = c % G[l]
            n_dest, n_part = max(1, W[l] // N), max(1, N // W[l])
            for i in range(n_dest):
                if W[l] >= N:
                    z_to = q * n_dest + i
                    src = turned[l].at[pl.ds(i * N, N)]
                    dst = at(f"B{l}").at[z]
                else:
                    z_to = q // n_part
                    src = turned[l]
                    low = pl.multiple_of((q % n_part) * W[l], W[l])
                    dst = at(f"B{l}").at[z, pl.ds(low, W[l])]
                ssem, rsem = at(f"Bs{l}").at[i], at(f"Br{l}").at[z]
                send_or_copy(src, dst, ssem, rsem, z_to, c, z_to == z)

        def rhs_part(l, part):
            if W[l] >= N:
                return at(f"B{l}")
            return at(f"B{l}").at[:, pl.ds(pl.multiple_of(part * W[l], W[l]), W[l])]

        def spread_rhs(l):
            q = c % G[l]
            n_dest, n_part = max(1, W[l] // N), max(1, N // W[l])
            holds = z // n_dest == q // n_part
            part = q % n_part
            here = rhs_part(l, part)

            def copy_to(m):
                return remote(
                    here, here, at(f"Ds{l}").at[m], at(f"Dr{l}").at[part], z, flipped(c, m)
                )

            @pl.when(holds)
            def _():
                for r in range(R):
                    block = at(f"B{l}").at[r]
                    if n_part > 1:
                        low = pl.multiple_of(part * W[l], W[l])
                        block = at(f"B{l}").at[r, pl.ds(low, W[l])]
                    arrived(block, at(f"Br{l}").at[r])
                for m in range(1, G[l]):
                    copy_to(m).start()

            def finish():
                @pl.when(holds)
                def _():
                    for m in range(1, G[l]):
                        copy_to(m).wait_send()

            sent.append(finish)

        def wait_rhs(l):
            q = c % G[l]
            n_dest, n_part = max(1, W[l] // N), max(1, N // W[l])
            for part in range(n_part):
                @pl.when(z // n_dest * n_part + part != q)
                def _():
                    arrived(rhs_part(l, part), at(f"Dr{l}").at[part])

        def z_block(l, index):
            return at(f"Z{l}").at[index]

        def c_block(l, index):
            return at(f"C{l}").at[pl.ds(pl.multiple_of(index * K[l], 16), K[l])]

        kinds = {"Z": (inverse, z_block), "C": (coupling, c_block)}

        def start_line(kind, l):
            source, block = kinds[kind]
            src, dst = source[l], block(l, z)
            pltpu.make_async_copy(src, dst, at(f"{kind}r{l}").at[0, 0]).start()
            for way, step in ((0, 1), (1, -1)):
                go_on(kind, l, way, step, 0, src, z)

        def go_on(kind, l, way, step, d, src, origin):
            open_end = jnp.logical_and(z + step >= 0, z + step < R)
            begun = jnp.logical_and(z - d * step >= 0, z - d * step < R)
            ready = jnp.logical_and(open_end, begun)
            dst = kinds[kind][1](l, origin)

            def copy():
                return remote(
                    src, dst, at(f"{kind}s{l}").at[way, d], at(f"{kind}r{l}").at[way, d + 1],
                    (z + step + R) % R, c,
                )

            @pl.when(ready)
            def _():
                copy().start()

            def finish():
                @pl.when(ready)
                def _():
                    copy().wait_send()

            sent.append(finish)

        def pass_line(kind, l, d):
            for way, step in ((0, 1), (1, -1)):
                origin = (z - d * step + R) % R
                block = kinds[kind][1](l, origin)
                begun = jnp.logical_and(z - d * step >= 0, z - d * step < R)

                @pl.when(begun)
                def _():
                    arrived(block, at(f"{kind}r{l}").at[way, d])

                if d < R - 1:
                    go_on(kind, l, way, step, d, block, origin)

        def pass_both(l, d):
            pass_line("Z", l, d)
            if l:
                pass_line("C", l, d)

        def own_line(kind, l):
            arrived(kinds[kind][1](l, z), at(f"{kind}r{l}").at[0, 0])

        def scatter(name, l, landed, ssem, rsem):
            q = c % G[l]
            for m in range(1, G[l]):
                send(
                    at(name).at[flipped(q, m)], at(landed).at[m],
                    at(ssem).at[m], at(rsem).at[m], z, flipped(c, m),
                )

        def total(name, l, landed, rsem):
            value = at(name)[c % G[l]].astype(jnp.float32)
            for m in range(1, G[l]):
                arrived(at(landed).at[m], at(rsem).at[m])
                value = value + at(landed)[m].astype(jnp.float32)
            return value

        def share_solution(l):
            q = c % G[l]
            here = at(f"xs{l}").at[q]
            for m in range(1, G[l]):
                send(here, here, at(f"xss{l}").at[m], at(f"xsr{l}").at[m], z, flipped(c, m))

        def wait_solution(l):
            q = c % G[l]
            for m in range(1, G[l]):
                arrived(at(f"xs{l}").at[flipped(q, m)], at(f"xsr{l}").at[m])

        def share_update(l):
            child, q = (c // G[l]) % 2, c % G[l]
            here = at(f"u{l}").at[child, q]
            for m in range(1, 2 * G[l]):
                send(here, here, at(f"us{l}").at[m], at(f"ur{l}").at[m], z, flipped(c, m))

        def wait_update(l):
            for m in range(1, 2 * G[l]):
                other = flipped(c, m)
                arrived(
                    at(f"u{l}").at[(other // G[l]) % 2, other % G[l]], at(f"ur{l}").at[m]
                )

        def make_table(l):
            front = c // G[l]
            step = K[l]
            for child in range(2):
                row = maps[l + 1][pl.ds(2 * front + child, 1), :]

                def body(i, carry):
                    start = pl.multiple_of(i * step, 16)
                    at_row = lax.broadcasted_iota(jnp.int32, (step, S[l + 1]), 0) + start
                    at(f"hot{l}")[child, pl.ds(start, step), :] = jnp.where(
                        at_row == row, 1.0, 0.0
                    ).astype(bf)
                    return carry

                lax.fori_loop(0, plan.total(l) // step, body, 0)

        def start_out(l):
            q = c % G[l]
            n_dest, n_part = max(1, W[l] // N), max(1, N // W[l])
            if W[l] >= N:
                holds = z // n_dest == q
                index = z % n_dest
                dst = at(f"oT{l}").at[pl.ds(pl.multiple_of(index * N, N), N)]
            else:
                holds = q // n_part == z
                index = 0
                dst = at(f"oT{l}")

            def piece(r):
                if W[l] >= N:
                    return at(f"fx{l}").at[r]
                low = pl.multiple_of((q % n_part) * W[l], W[l])
                return at(f"fx{l}").at[r, pl.ds(low, W[l])]

            def copy_to(d):
                r = (z + d) % R
                return remote(
                    piece(r), dst, at(f"Os{l}").at[d], at(f"Or{l}").at[index], r, c
                )

            @pl.when(holds)
            def _():
                pltpu.make_async_copy(piece(z), dst, at(f"Or{l}").at[index]).start()
                for d in range(1, R):
                    copy_to(d).start()

            def finish():
                @pl.when(holds)
                def _():
                    for d in range(1, R):
                        copy_to(d).wait_send()

            sent.append(finish)

        def finish_out(l):
            if W[l] >= N:
                for i in range(W[l] // N):
                    arrived(at(f"oT{l}").at[pl.ds(i * N, N)], at(f"Or{l}").at[i])
            else:
                arrived(at(f"oT{l}"), at(f"Or{l}").at[0])
            if narrow(W[l]):
                outs[l][...] = at(f"oT{l}")[...]
            else:
                outs[l][...] = dot_nt(eye(K[l]), at(f"oT{l}")[...]).astype(bf)

        def pivot(l, blocks):
            product = dot_nn if narrow(K[l]) else dot_nt
            value = product(blocks[0], at(f"Z{l}")[0])
            for r in range(1, R):
                value = value + product(blocks[r], at(f"Z{l}")[r])
            at(f"y{l}")[...] = value.astype(bf)

        start_line("Z", 3)
        start_line("C", 3)
        start_rhs(3)
        start_line("Z", 2)
        for l in (2, 1, 0):
            start_rhs(l)
        make_table(2)
        pass_both(3, 1)
        start_line("C", 2)
        for d in range(2, R):
            pass_both(3, d)
            if d == 2:
                pass_both(2, 1)
                start_line("Z", 1)
        for l in (2, 1, 0):
            spread_rhs(l)
        spread_rhs(3)
        own_line("Z", 3)
        pivot(3, [at("B3")[r] for r in range(R)])
        own_line("C", 3)
        at("u3")[(c // G[3]) % 2, 0] = (-dot_nt(at("y3")[...], at("C3")[...])).astype(bf)
        share_update(3)
        pass_both(2, 2)
        start_line("C", 1)
        pass_line("Z", 1, 1)
        make_table(1)
        for d in range(3, R):
            pass_both(2, d)

        for l in (2, 1, 0):
            wait_update(l + 1)
            pair = [at(f"u{l + 1}")[child].reshape(N, S[l + 1]) for child in range(2)]

            def assembled(low, size):
                value = dot_nt(pair[0], at(f"hot{l}")[0, low:low + size, :])
                return value + dot_nt(pair[1], at(f"hot{l}")[1, low:low + size, :])

            wait_rhs(l)
            blocks = [
                (at(f"B{l}")[r].astype(jnp.float32) + assembled(r * K[l], K[l])).astype(bf)
                for r in range(R)
            ]
            if l == 1:
                for d in range(3, R):
                    pass_both(1, d)
                pass_line("Z", 0, 2)
            if l == 0:
                for d in range(3, R):
                    pass_line("Z", 0, d)
            own_line("Z", l)
            pivot(l, blocks)
            if l:
                own_line("C", l)
                share = (G[l], N // G[l], S[l])
                at(f"up{l}")[...] = (
                    dot_nt(at(f"y{l}")[...], at(f"C{l}")[...]).astype(bf).reshape(share)
                )
                scatter(f"up{l}", l, f"ut{l}", f"ups{l}", f"upr{l}")
                if l == 2:
                    pass_line("C", 1, 1)
                    start_line("Z", 0)
                    pass_line("Z", 1, 2)
                    make_table(0)
                    pass_line("C", 1, 2)
                    pass_line("Z", 0, 1)
                at(f"H{l}")[...] = assembled(S[l], S[l]).astype(bf).reshape(share)
                reduced = total(f"up{l}", l, f"ut{l}", f"upr{l}")
                q = c % G[l]
                at(f"u{l}")[(c // G[l]) % 2, q] = (
                    at(f"H{l}")[q].astype(jnp.float32) - reduced
                ).astype(bf)
                share_update(l)

        per = G[0] // R
        lanes = S[0] // G[0]
        for r in range(R):
            product = dot_nt if narrow(K[0]) else dot_nn
            value = product(at("y0")[...], at("Z0")[r]).astype(bf)
            for i in range(per):
                at("xp0")[r * per + i] = value[:, i * lanes:(i + 1) * lanes]
        scatter("xp0", 0, "xr0", "xps0", "xpr0")
        at("xs0")[c % G[0]] = total("xp0", 0, "xr0", "xpr0").astype(bf)
        share_solution(0)
        wait_solution(0)
        for r in range(R):
            for i in range(per):
                at("fx0")[r, :, i * lanes:(i + 1) * lanes] = at("xs0")[r * per + i]
        start_out(0)

        for l in (1, 2, 3):
            child = (c // G[l]) % 2
            gathered = dot_nn(at(f"fx{l - 1}")[0], at(f"hot{l - 1}")[child, 0:K[l - 1], :])
            for r in range(1, R):
                gathered = gathered + dot_nn(
                    at(f"fx{l - 1}")[r],
                    at(f"hot{l - 1}")[child, r * K[l - 1]:(r + 1) * K[l - 1], :],
                )
            if l > 1:
                gathered = gathered + dot_nn(
                    at(f"v{l - 1}")[...], at(f"hot{l - 1}")[child, S[l - 1]:, :]
                )
            at(f"v{l}")[...] = gathered.astype(bf)
            residual = (
                at(f"y{l}")[...].astype(jnp.float32)
                - dot_nn(at(f"v{l}")[...], at(f"C{l}")[...])
            ).astype(bf)
            for r in range(R):
                product = dot_nt if narrow(K[l]) else dot_nn
                value = product(residual, at(f"Z{l}")[r]).astype(bf)
                if G[l] > 1:
                    at(f"xp{l}")[:, r] = value.reshape(G[l], N // G[l], K[l])
                else:
                    at(f"fx{l}")[r] = value
            if G[l] > 1:
                if G[l] == 2:
                    send(
                        at(f"xp{l}"), at(f"xr{l}"), at(f"xps{l}").at[1], at(f"xpr{l}").at[1],
                        z, flipped(c, 1),
                    )
                    arrived(at(f"xr{l}"), at(f"xpr{l}").at[1])
                    for r in range(R):
                        both = at(f"xp{l}")[:, r].astype(jnp.float32) + at(f"xr{l}")[:, r].astype(
                            jnp.float32
                        )
                        at(f"fx{l}")[r] = both.astype(bf).reshape(N, K[l])
                    start_out(l)
                    continue
                scatter(f"xp{l}", l, f"xr{l}", f"xps{l}", f"xpr{l}")
                if l == 1:
                    finish_out(0)
                at(f"xs{l}")[c % G[l]] = total(f"xp{l}", l, f"xr{l}", f"xpr{l}").astype(bf)
                share_solution(l)
                wait_solution(l)
                for r in range(R):
                    at(f"fx{l}")[r] = at(f"xs{l}")[:, r].reshape(N, K[l])
            start_out(l)
        for l in (1, 2, 3):
            finish_out(l)
        for finish in sent:
            finish()

    return kernel, scratch


def hand_on(*refs):
    for source, target in zip(refs[:4], refs[4:]):
        target[...] = source[...]


def fused_device(*blocks):
    plan = Plan(
        lax.axis_size("row"), lax.axis_size("col"),
        [block.shape for block in blocks[:4]], blocks[7].shape,
    )
    if not plan.fits():
        return per_device(*blocks)
    kernel, scratch = build_kernel(plan)
    blocks = list(blocks)
    for at in (0, 1, 2, 3, 7, 8, 9, 10):
        if narrow(blocks[at].shape[1]):
            blocks[at] = blocks[at].T
    vmem = pl.BlockSpec(memory_space=pltpu.VMEM)
    solved = pl.pallas_call(
        kernel,
        out_shape=tuple(jax.ShapeDtypeStruct(block.shape, block.dtype) for block in blocks[7:11]),
        in_specs=[vmem] * 14,
        out_specs=(vmem,) * 4,
        scratch_shapes=scratch,
        compiler_params=pltpu.CompilerParams(
            collective_id=0, has_side_effects=True, vmem_limit_bytes=56 * 2**20
        ),
    )(*blocks)
    solved = pl.pallas_call(
        hand_on,
        out_shape=tuple(jax.ShapeDtypeStruct(block.shape, block.dtype) for block in solved),
        in_specs=[vmem] * 4,
        out_specs=(vmem,) * 4,
    )(*solved)
    return tuple(
        block.T if narrow(width) else block for block, width in zip(solved, plan.width)
    )


def solution(mesh):
    in_specs = (
        P("col", "row"),
        P("col", "row"),
        P("col", "row"),
        P("col", "row"),
        P("row", "col"),
        P("row", "col"),
        P("row", "col"),
        P("row", "col"),
        P("row", "col"),
        P("row", "col"),
        P("row", "col"),
        P(),
        P(),
        P(),
    )
    out_specs = (P("row", "col"), P("row", "col"), P("row", "col"), P("row", "col"))
    return jax.shard_map(
        fused_device, mesh=mesh, in_specs=in_specs, out_specs=out_specs, check_vma=False
    )
```
